32 devices in a mesh: parts: 2 (over x), blk: 16 (over z, y, core).
Axes of the slice: x: 2, y: 2, z: 4, core: 2. Of those that a mesh axis runs over, the one named last changes fastest.
Arguments:
- particles: bfloat16 [4096, 4608], P(('parts', 'blk')), parts along dimension 0, may hold values from -24 to 24
- references: bfloat16 [64, 4608], P(('parts', 'blk')), parts along dimension 0, may hold values from -0.5 to 0.5
- inv_noise: float32 [4096], P(('parts', 'blk')), parts along dimension 0, may hold values from 1 to 4
- assign: int32 [4096, 2], P(('parts', 'blk')), parts along dimension 0, may hold values from 0 to 31, all different within a row; in each aligned block of 128 rows (0 to 127, 128 to 255, ...) at most 16 rows name the same one
Outputs:
- class_sums: float32 [64, 4608], P(('parts', 'blk')), parts along dimension 0
- class_mass: float32 [64], P(('parts', 'blk')), parts along dimension 0
- log_evidence: float32 [4096], P(('parts', 'blk')), parts along dimension 0
The draws below stay inside these ranges and needn't reach their ends.
There are 2 independent parts, one for each index of `parts`. The reference program is written for one: setup_inputs(seed, part) draws one part's arguments, and reference() takes and returns one part's arrays. A program takes and returns all parts, laid end to end along the dimension named above; each array names one. Nothing has to cross between parts.
Inputs may be any that keep to these rules, and one draw needn't show every extreme that they name: `assign`: among the rows of one device, at most 16 name any one class; in every draw some device's block reaches this bound.
All inputs are finite; a program needn't handle non-finite values.
Results may differ from the reference program's by a relative error of at most 0.0039.
Values may be sent and summed in bfloat16 or wider, within the bound.
No kernel may reach another device: no remote copies, remote signals or barrier semaphores. Data moves between devices by JAX's collectives and lax.ppermute only.
A program may use at most 128 MiB of HBM per device.

```python
import math
import jax
import jax.numpy as jnp
import numpy as np

P_DEV = 128
ROT = 12
TOPK = 2
CYCLES = 12
ANGLES = 384
F = 4608
CLASSES = 32
PARTICLES = 2048
MOST = 16


def class_shapes(key):
    scales = jnp.exp(jax.random.uniform(jax.random.fold_in(key, 11), (CLASSES,), jnp.float32, math.log(0.5), math.log(2.0)))
    normal_part = jnp.clip(jax.random.normal(jax.random.fold_in(key, 12), (CLASSES, F), jnp.float32), -4.0, 4.0)
    shaped = jnp.clip(normal_part * scales[:, None] * F ** (-0.5), -0.5, 0.5)
    return shaped


def draw_references(key, part):
    return class_shapes(key).astype(jnp.bfloat16)


def draw_particles(key, part):
    values = jnp.clip(jax.random.normal(jax.random.fold_in(key, 22), (PARTICLES, F), jnp.float32), -6.0, 6.0)
    values = jnp.clip(values, -24.0, 24.0)
    return values.astype(jnp.bfloat16)


def block_levels(key, extent, pieces, low, high):
    gain = 1.0
    for axis_at, blocks in pieces:
        steps = jax.random.uniform(jax.random.fold_in(jax.random.fold_in(key, 6), axis_at), (blocks,), jnp.float32, low / len(pieces), high / len(pieces))
        gain = gain * jnp.repeat(jnp.exp(steps), extent[axis_at] // blocks).reshape((-1,) + (1,) * (len(extent) - 1 - axis_at))
    return gain


def assign_block(rng, own, number, rows, count, top, most, slope):
    ranking = jax.random.permutation(rng, count)
    heavy_load, common = portions_of(count, rows * top, most, slope, True), portions_of(count, rows * top, most, slope, False)
    places = jnp.arange(count)

    def named(sizes, offset_by):
        used = int((sizes > 0).sum())
        fixed = max(1, used // 4)
        passed = fixed + (places - fixed + offset_by * (used - fixed)) % max(1, count - fixed)
        return jnp.zeros((count,), jnp.int32).at[ranking[jnp.where(places < fixed, places, passed)]].set(jnp.asarray(sizes, jnp.int32))

    sizes = jnp.where(number % 4 == 0, named(heavy_load, number // 4), named(common, number - number // 4 - 1))
    mixed = jax.random.permutation(jax.random.fold_in(own, 3), count)
    donor, receiver = mixed[0:count // 2 * 2:2], mixed[1:count // 2 * 2:2]
    room = jnp.minimum(sizes[donor] - 1, most - sizes[receiver]) // 2
    room = jnp.where((donor == ranking[0]) | (receiver == ranking[0]) | (sizes[receiver] == 0), 0, jnp.maximum(room, 0))
    passed = jax.random.randint(jax.random.fold_in(own, 4), (count // 2,), 0, 1 << 20) % (room + 1)
    sizes = sizes.at[donor].add(-passed).at[receiver].add(passed)
    members = jnp.searchsorted(jnp.cumsum(sizes), jnp.arange(rows * top), side="right").astype(jnp.int32)
    listing = members.reshape(top, rows).T
    listing = listing[jax.random.permutation(jax.random.fold_in(own, 1), rows)]
    offset_by = jax.random.randint(jax.random.fold_in(own, 2), (rows, 1), 0, top)
    return jnp.take_along_axis(listing, (jnp.arange(top)[None, :] + offset_by) % top, axis=1)


def portions_of(count, total, reach, lean, full):
    loads = [(1 << 20) // math.isqrt(rank ** lean) + 1 for rank in range(1, count + 1)]
    largest = reach if full else min(reach, max(-(-total // count), total * loads[0] // sum(loads)))
    least = 1 if total - largest >= count - 1 else 0
    counts, spare = [largest] + [least] * (count - 1), total - largest - least * (count - 1)
    while spare > 0:
        candidates = [i for i in range(1, count) if counts[i] < largest] or [i for i in range(1, count) if counts[i] < reach]
        whole, remaining = sum([loads[i] for i in candidates]), spare
        for i in candidates:
            more = min(reach - counts[i], max(1, remaining * loads[i] // whole), spare)
            counts[i] = counts[i] + more
            spare = spare - more
    return np.array(counts)


def setup_inputs(seed: int = 0, part: int = 0) -> dict:
    key_of = jax.random.split(jax.random.key(seed), 5)
    part_keys = jax.random.split(jax.random.fold_in(key_of[4], part), 5)
    particles = draw_particles(jax.random.fold_in(jax.random.fold_in(key_of[4], part), 71), part)
    references = draw_references(jax.random.fold_in(jax.random.fold_in(key_of[4], part), 71), part)
    inv_noise = jnp.clip(jnp.exp(math.log(4.0) - 1.3862944 * jax.random.uniform(part_keys[2], (PARTICLES,), jnp.float32) ** block_levels(part_keys[2], (PARTICLES,), ((0, 16),), -0.2, 0.2)), 1.0, 4.0)
    assign_keys = jax.random.split(jax.random.fold_in(part_keys[3], 1), PARTICLES // P_DEV)
    assign_turns = jax.random.permutation(jax.random.fold_in(part_keys[3], 3), PARTICLES // P_DEV)
    assign = jax.vmap(lambda own, number: assign_block(jax.random.fold_in(part_keys[3], 2), own, number, P_DEV, CLASSES, TOPK, MOST, 1))(assign_keys, assign_turns).reshape((PARTICLES, TOPK))
    return {"particles": particles, "references": references, "inv_noise": inv_noise, "assign": assign}


def turn_all(cube, sign):
    step = ANGLES // ROT
    return jnp.stack([jnp.roll(cube, sign * r * step, axis=2) for r in range(ROT)], axis=1)


def reference(particles, references, inv_noise, assign):
    cube = references.reshape(CLASSES, CYCLES, ANGLES)
    turned = turn_all(cube, 1).reshape(CLASSES * ROT, F)
    energy = jnp.sum(jnp.square(references.astype(jnp.float32)), axis=1)
    dots = jnp.dot(particles, turned.T, preferred_element_type=jnp.float32)
    logits = inv_noise[:, None] * (dots - 0.5 * jnp.repeat(energy, ROT)[None, :])
    top = jnp.max(logits, axis=1, keepdims=True)
    total = jnp.sum(jnp.exp(logits - top), axis=1, keepdims=True)
    log_evidence = top + jnp.log(total)
    post = jnp.exp(logits - log_evidence).reshape(PARTICLES, CLASSES, ROT)
    picked = jnp.take_along_axis(post, assign[:, :, None].astype(jnp.int32), axis=1)
    pcube = particles.reshape(PARTICLES, CYCLES, ANGLES)
    step = ANGLES // ROT
    rows = jnp.zeros((PARTICLES, TOPK, F), jnp.float32)
    for r in range(ROT):
        back = jnp.roll(pcube, -r * step, axis=2).reshape(PARTICLES, 1, F).astype(jnp.float32)
        rows = rows + picked[:, :, r, None] * back
    rows = rows.astype(jnp.bfloat16).reshape(PARTICLES * TOPK, F)
    weights = jnp.sum(picked, axis=2).astype(jnp.bfloat16).reshape(PARTICLES * TOPK)
    flat = assign.reshape(PARTICLES * TOPK)
    class_sums = jax.ops.segment_sum(rows.astype(jnp.float32), flat, CLASSES)
    class_mass = jax.ops.segment_sum(weights.astype(jnp.float32), flat, CLASSES)
    return class_sums, class_mass, log_evidence[:, 0]
```

```python
import functools

import jax
import jax.numpy as jnp
from jax import lax
from jax.experimental import pallas as pl
from jax.experimental.pallas import tpu as pltpu
from jax.sharding import PartitionSpec as P

ROT = 12
CYCLES = 12
ANGLES = 384
LANES = 128
STEP = ANGLES // ROT
FINE = LANES // STEP
COARSE = ROT // FINE


def assign_kernel(bits, p_ref, refs_ref, noise_ref, assign_ref, keep_ref, send_ref, log_ref, turned_ref):
    classes = refs_ref.shape[0]
    owned = classes >> bits
    half = classes // 2
    group = FINE * classes
    me = lax.axis_index("blk")

    energy = jnp.zeros((classes, LANES), jnp.float32)
    for c in range(CYCLES):
        cube = refs_ref[:, c * ANGLES:(c + 1) * ANGLES].astype(jnp.float32)
        for v in range(COARSE):
            piece = cube[:, v * LANES:(v + 1) * LANES]
            energy = energy + piece * piece
        for s in range(FINE):
            moved = (cube if s == 0 else pltpu.roll(cube, s * STEP, 1)).astype(jnp.bfloat16)
            for q in range(COARSE):
                for v in range(COARSE):
                    at = c * ANGLES + (v + q) % COARSE * LANES
                    turned_ref[q * group + s * classes:q * group + (s + 1) * classes, at:at + LANES] = (
                        moved[:, v * LANES:(v + 1) * LANES]
                    )
    energy = jnp.sum(energy, axis=1, keepdims=True)

    dots = lax.dot_general(
        turned_ref[...], p_ref[...], (((1,), (1,)), ((), ())), preferred_element_type=jnp.float32
    )
    rows = dots.shape[1]
    dots = dots.reshape(ROT, classes, rows)
    logits = noise_ref[...][None] * (dots - 0.5 * energy[None])
    top = jnp.max(jnp.max(logits, axis=0), axis=0, keepdims=True)
    grown = jnp.exp(logits - top[None])
    total = jnp.sum(jnp.sum(grown, axis=0), axis=0, keepdims=True)
    log_ref[...] = top + jnp.log(total)

    row = lax.broadcasted_iota(jnp.int32, (classes, rows), 0)
    place = row // owned
    mixed = jnp.zeros_like(place)
    for i in range(bits):
        mixed = mixed + (((place >> i) & 1) << (bits - 1 - i))
    ident = (mixed ^ me) * owned + row % owned
    named = (ident == assign_ref[0:1, :]) | (ident == assign_ref[1:2, :])
    scale = jnp.where(named, 1.0 / total, 0.0)
    post = grown * scale[None]
    weights = jnp.sum(post, axis=0).astype(jnp.bfloat16).astype(jnp.float32)
    mass = jnp.broadcast_to(jnp.sum(weights, axis=1, keepdims=True), (classes, LANES))

    post = post.reshape(COARSE, group, rows)
    post = jnp.concatenate([post[q] for q in range(COARSE)], axis=1)
    high = post.astype(jnp.bfloat16)
    low = (post - high.astype(jnp.float32)).astype(jnp.bfloat16)
    both = jnp.concatenate([high, low], axis=0)
    for c in range(CYCLES):
        pieces = [p_ref[:, c * ANGLES + v * LANES:c * ANGLES + (v + 1) * LANES] for v in range(COARSE)]
        stacked = jnp.concatenate(
            [jnp.concatenate([pieces[(v + q) % COARSE] for v in range(COARSE)], axis=1) for q in range(COARSE)],
            axis=0,
        )
        part = jnp.dot(both, stacked, preferred_element_type=jnp.float32)
        part = part[:group] + part[group:]
        summed = part[(FINE - 1) * classes:]
        for s in range(FINE - 2, -1, -1):
            summed = part[s * classes:(s + 1) * classes] + pltpu.roll(summed, ANGLES - STEP, 1)
        keep_ref[:, c * ANGLES:(c + 1) * ANGLES] = summed[:half]
        send_ref[:, c * ANGLES:(c + 1) * ANGLES] = summed[half:].astype(jnp.bfloat16)
    width = CYCLES * ANGLES
    keep_ref[:, width:] = mass[:half]
    send_ref[:, width:] = mass[half:].astype(jnp.bfloat16)


def local(particles, references, inv_noise, assign):
    rows, width = particles.shape
    owned = references.shape[0]
    devices = lax.axis_size("blk")
    bits = devices.bit_length() - 1
    classes = owned * devices

    def swap(x, bit):
        return lax.ppermute(x, "blk", [(i, i ^ bit) for i in range(devices)])

    gathered = references
    for b in range(bits - 1, -1, -1):
        gathered = jnp.concatenate([gathered, swap(gathered, 1 << b)], axis=0)

    half = classes // 2
    wide = width + LANES
    keep, send, log_evidence = pl.pallas_call(
        functools.partial(assign_kernel, bits),
        out_shape=(
            jax.ShapeDtypeStruct((half, wide), jnp.float32),
            jax.ShapeDtypeStruct((half, wide), jnp.bfloat16),
            jax.ShapeDtypeStruct((1, rows), jnp.float32),
        ),
        in_specs=[pl.BlockSpec(memory_space=pltpu.VMEM)] * 4,
        out_specs=[pl.BlockSpec(memory_space=pltpu.VMEM)] * 3,
        scratch_shapes=[pltpu.VMEM((ROT * classes, width), jnp.bfloat16)],
        compiler_params=pltpu.CompilerParams(vmem_limit_bytes=48 * 1024 * 1024),
    )(particles, gathered, inv_noise[None, :], assign.T)

    for b in range(bits):
        total = keep + swap(send, 1 << b).astype(jnp.float32)
        part = total.shape[0] // 2
        if b < bits - 1:
            keep, send = total[:part], total[part:].astype(jnp.bfloat16)
    return total[:, :width], total[:, width], log_evidence[0]


def solution(mesh):
    placed = (
        P(("parts", "blk"), None),
        P(("parts", "blk"), None),
        P(("parts", "blk")),
        P(("parts", "blk"), None),
    )
    return jax.shard_map(
        local,
        mesh=mesh,
        in_specs=placed,
        out_specs=(P(("parts", "blk"), None), P(("parts", "blk")), P(("parts", "blk"))),
        check_vma=False,
    )
```

```python
import functools

import jax
import jax.numpy as jnp
from jax import lax
from jax.experimental import pallas as pl
from jax.experimental.pallas import tpu as pltpu
from jax.sharding import PartitionSpec as P

ROT = 12
CYCLES = 12
ANGLES = 384
WIDTH = CYCLES * ANGLES
LANES = 128
STEP = ANGLES // ROT
FINE = LANES // STEP
COARSE = ROT // FINE
VMEM = pl.BlockSpec(memory_space=pltpu.VMEM)
HBM = pl.BlockSpec(memory_space=pltpu.HBM)
PARAMS = pltpu.CompilerParams(vmem_limit_bytes=40 * 1024 * 1024)


def stage_kernel(refs_ref, out_ref):
    out_ref[...] = refs_ref[...]


def score(refs_ref, p_ref, noise, turned_ref):
    classes = refs_ref.shape[0]
    group = FINE * classes
    energy = jnp.zeros((classes, LANES), jnp.float32)
    for c in range(CYCLES):
        cube = refs_ref[:, c * ANGLES:(c + 1) * ANGLES].astype(jnp.float32)
        for v in range(COARSE):
            piece = cube[:, v * LANES:(v + 1) * LANES]
            energy = energy + piece * piece
        moved = [cube] + [pltpu.roll(cube, s * STEP, 1) for s in range(1, FINE)]
        moved = jnp.concatenate(moved, axis=0).astype(jnp.bfloat16)
        for q in range(COARSE):
            for v in range(COARSE):
                at = c * ANGLES + (v + q) % COARSE * LANES
                turned_ref[q * group:(q + 1) * group, at:at + LANES] = moved[:, v * LANES:(v + 1) * LANES]
    energy = jnp.sum(energy, axis=1, keepdims=True)
    dots = lax.dot_general(
        turned_ref[...], p_ref[...], (((1,), (1,)), ((), ())), preferred_element_type=jnp.float32
    )
    dots = dots.reshape(ROT, classes, dots.shape[1])
    return noise[None] * (dots - 0.5 * energy[None])


def early_kernel(p_own, p_far, noise_own, noise_far, name_own, name_far, refs_ref,
                 p_ref, noise_ref, name_ref, logits_ref, turned_ref, sems):
    rows = p_own.shape[0]
    copies = [
        pltpu.make_async_copy(p_own, p_ref.at[0:rows], sems.at[0]),
        pltpu.make_async_copy(p_far, p_ref.at[rows:2 * rows], sems.at[1]),
        pltpu.make_async_copy(noise_own, noise_ref.at[:, 0:rows], sems.at[2]),
        pltpu.make_async_copy(noise_far, noise_ref.at[:, rows:2 * rows], sems.at[3]),
        pltpu.make_async_copy(name_own, name_ref.at[:, 0:rows], sems.at[4]),
        pltpu.make_async_copy(name_far, name_ref.at[:, rows:2 * rows], sems.at[5]),
    ]
    for copy in copies:
        copy.start()
    for copy in copies:
        copy.wait()
    logits_ref[...] = score(refs_ref, p_ref, noise_ref[...], turned_ref)


def late_kernel(refs_ref, p_ref, noise_ref, early_ref, logits_ref, part_ref, turned_ref):
    late = score(refs_ref, p_ref, noise_ref[...], turned_ref)
    logits_ref[...] = late
    early = early_ref[...]
    top = jnp.maximum(jnp.max(late, axis=0), jnp.max(early, axis=0))
    top = jnp.max(top, axis=0, keepdims=True)
    total = jnp.sum(jnp.exp(late - top[None]), axis=0) + jnp.sum(jnp.exp(early - top[None]), axis=0)
    part_ref[...] = top + jnp.log(jnp.sum(total, axis=0, keepdims=True))


def back_kernel(bits, owned, first, logits_ref, near_ref, far_ref, name_ref, p_ref, sums_ref, log_ref=None):
    classes, rows = logits_ref.shape[1:]
    me = lax.axis_index("blk")
    near, far = near_ref[...], far_ref[...]
    top = jnp.maximum(near, far)
    log_evidence = top + jnp.log(jnp.exp(near - top) + jnp.exp(far - top))
    if log_ref is not None:
        log_ref[...] = log_evidence[:, :log_ref.shape[1]]

    row = lax.broadcasted_iota(jnp.int32, (classes, rows), 0) + first
    place = row // owned
    mixed = jnp.zeros_like(place)
    for i in range(bits - 1):
        mixed = mixed + (((place >> i) & 1) << (bits - 1 - i))
    ident = (mixed ^ me) * owned + row % owned
    named = (ident == name_ref[0:1, :]) | (ident == name_ref[1:2, :])
    post = jnp.where(named[None], jnp.exp(logits_ref[...] - log_evidence[None]), 0.0)
    weights = jnp.sum(post, axis=0).astype(jnp.bfloat16).astype(jnp.float32)
    mass = jnp.broadcast_to(jnp.sum(weights, axis=1, keepdims=True), (classes, LANES))
    sums_ref[:, WIDTH:] = mass.astype(sums_ref.dtype)

    count = ROT * classes
    post = post.reshape(count, rows)
    high = post.astype(jnp.bfloat16)
    low = (post - high.astype(jnp.float32)).astype(jnp.bfloat16)
    both = jnp.concatenate([high, low], axis=0)
    group = FINE * classes
    for c in range(0, CYCLES, 2):
        part = jnp.dot(both, p_ref[:, c * ANGLES:(c + 2) * ANGLES], preferred_element_type=jnp.float32)
        part = part[:count] + part[count:]
        for d in range(2):
            blocks = []
            for v in range(COARSE):
                block = None
                for q in range(COARSE):
                    at = d * ANGLES + (v + q) % COARSE * LANES
                    piece = part[q * group:(q + 1) * group, at:at + LANES]
                    block = piece if block is None else block + piece
                blocks.append(block)
            turned = jnp.concatenate(blocks, axis=1)
            summed = turned[(FINE - 1) * classes:]
            for s in range(FINE - 2, -1, -1):
                summed = turned[s * classes:(s + 1) * classes] + pltpu.roll(summed, ANGLES - STEP, 1)
            sums_ref[:, (c + d) * ANGLES:(c + d + 1) * ANGLES] = summed.astype(sums_ref.dtype)


def last_kernel(keep_ref, got_ref, sums_ref, mass_ref):
    owned = sums_ref.shape[0]
    total = keep_ref[0:owned, :] + got_ref[...].astype(jnp.float32)
    sums_ref[...] = total[:, :WIDTH]
    for i in range(owned):
        mass_ref[i] = total[i, WIDTH]


def local(particles, references, inv_noise, assign):
    rows, width = particles.shape
    owned = references.shape[0]
    devices = lax.axis_size("blk")
    bits = devices.bit_length() - 1
    half = owned * devices // 4
    both = 2 * rows
    wide = width + LANES
    f32, bf16 = jnp.float32, jnp.bfloat16

    def swap(x, bit):
        return lax.ppermute(x, "blk", [(i, i ^ bit) for i in range(devices)])

    noise, names = inv_noise[None, :], assign.T
    p_far, noise_far, names_far = swap(particles, 1), swap(noise, 1), swap(names, 1)

    own = pl.pallas_call(
        stage_kernel, out_shape=jax.ShapeDtypeStruct((owned, width), bf16),
        in_specs=[VMEM], out_specs=VMEM, compiler_params=PARAMS, name="stage",
    )(references)
    gathered = references
    for b in range(bits - 1, 0, -1):
        got = swap(gathered, 1 << b)
        if b == bits - 1:
            gathered = own
        if b > 1:
            gathered = jnp.concatenate([gathered, got], axis=0)

    turned = pltpu.VMEM((ROT * half, width), bf16)
    score_cost = pl.CostEstimate(
        flops=2 * ROT * half * both * width, bytes_accessed=4 * both * width, transcendentals=0)
    p_all, noise_all, names_all, early = pl.pallas_call(
        early_kernel,
        out_shape=(
            jax.ShapeDtypeStruct((both, width), bf16),
            jax.ShapeDtypeStruct((1, both), f32),
            jax.ShapeDtypeStruct((2, both), jnp.int32),
            jax.ShapeDtypeStruct((ROT, half, both), f32),
        ),
        in_specs=[HBM] * 6 + [VMEM],
        out_specs=[VMEM] * 4,
        scratch_shapes=[turned, pltpu.SemaphoreType.DMA((6,))],
        compiler_params=PARAMS, cost_estimate=score_cost, name="early",
    )(particles, p_far, noise, noise_far, names, names_far, gathered)
    late, near = pl.pallas_call(
        late_kernel,
        out_shape=(jax.ShapeDtypeStruct((ROT, half, both), f32), jax.ShapeDtypeStruct((1, both), f32)),
        in_specs=[VMEM] * 4,
        out_specs=[VMEM] * 2,
        scratch_shapes=[turned],
        compiler_params=PARAMS, cost_estimate=score_cost, name="late",
    )(got, p_all, noise_all, early)
    far = swap(near, 1)
    far = jnp.concatenate([far[:, rows:], far[:, :rows]], axis=1)

    send = pl.pallas_call(
        functools.partial(back_kernel, bits, owned, half),
        out_shape=jax.ShapeDtypeStruct((half, wide), bf16),
        in_specs=[VMEM] * 5,
        out_specs=VMEM,
        compiler_params=PARAMS, cost_estimate=score_cost, name="back_send",
    )(late, near, far, names_all, p_all)
    keep, log_evidence = pl.pallas_call(
        functools.partial(back_kernel, bits, owned, 0),
        out_shape=(jax.ShapeDtypeStruct((half, wide), f32), jax.ShapeDtypeStruct((1, rows), f32)),
        in_specs=[VMEM] * 5,
        out_specs=[VMEM] * 2,
        compiler_params=PARAMS, cost_estimate=score_cost, name="back_keep",
    )(early, near, far, names_all, p_all)

    for b in range(1, bits):
        got = swap(send, 1 << b)
        if b < bits - 1:
            total = keep + got.astype(f32)
            part = total.shape[0] // 2
            keep, send = total[:part], total[part:].astype(bf16)
    sums, mass = pl.pallas_call(
        last_kernel,
        out_shape=(jax.ShapeDtypeStruct((owned, width), f32), jax.ShapeDtypeStruct((owned,), f32)),
        in_specs=[VMEM] * 2,
        out_specs=[VMEM, pl.BlockSpec(memory_space=pltpu.SMEM)],
        compiler_params=PARAMS, name="last",
    )(keep, got)
    return sums, mass, log_evidence[0]


def solution(mesh):
    placed = (
        P(("parts", "blk"), None),
        P(("parts", "blk"), None),
        P(("parts", "blk")),
        P(("parts", "blk"), None),
    )
    return jax.shard_map(
        local,
        mesh=mesh,
        in_specs=placed,
        out_specs=(P(("parts", "blk"), None), P(("parts", "blk")), P(("parts", "blk"))),
        check_vma=False,
    )
```

```python
import functools

import jax
import jax.numpy as jnp
from jax import lax
from jax.experimental import pallas as pl
from jax.experimental.pallas import tpu as pltpu
from jax.sharding import PartitionSpec as P

ROT = 12
CYCLES = 12
ANGLES = 384
TOPK = 2
WIDTH = CYCLES * ANGLES
LANES = 128
STEP = ANGLES // ROT
FINE = LANES // STEP
COARSE = ROT // FINE
VMEM = pl.BlockSpec(memory_space=pltpu.VMEM)
HBM = pl.BlockSpec(memory_space=pltpu.HBM)
PARAMS = pltpu.CompilerParams(vmem_limit_bytes=40 * 1024 * 1024)


def stage_kernel(refs, particles, noise, names, refs_ref, p_ref, packed_ref, noise_ref, names_ref, sems):
    copies = [
        pltpu.make_async_copy(src, dst, sems.at[i])
        for i, (src, dst) in enumerate(
            ((refs, refs_ref), (noise, noise_ref), (names, names_ref), (particles, p_ref))
        )
    ]
    for copy in copies:
        copy.start()
    for copy in copies[:3]:
        copy.wait()
    packed_ref[0:1, :] = noise_ref[...]
    packed_ref[1:1 + TOPK, :] = names_ref[...].astype(jnp.float32)
    copies[3].wait()


def particles_of(own_ref, far_ref, start, size):
    return jnp.concatenate([own_ref[:, start:start + size], far_ref[:, start:start + size]], axis=0)


def score(refs_ref, own_ref, far_ref, near_info, far_info, turned_ref):
    classes = refs_ref.shape[0]
    group = FINE * classes
    energy = jnp.zeros((classes, LANES), jnp.float32)
    for c in range(CYCLES):
        cube = refs_ref[:, c * ANGLES:(c + 1) * ANGLES].astype(jnp.float32)
        for v in range(COARSE):
            piece = cube[:, v * LANES:(v + 1) * LANES]
            energy = energy + piece * piece
        moved = [cube] + [pltpu.roll(cube, s * STEP, 1) for s in range(1, FINE)]
        moved = jnp.concatenate(moved, axis=0).astype(jnp.bfloat16)
        for q in range(COARSE):
            for v in range(COARSE):
                at = c * ANGLES + (v + q) % COARSE * LANES
                turned_ref[q * group:(q + 1) * group, at:at + LANES] = moved[:, v * LANES:(v + 1) * LANES]
    energy = jnp.sum(energy, axis=1, keepdims=True)
    dots = lax.dot_general(
        turned_ref[...], particles_of(own_ref, far_ref, 0, WIDTH), (((1,), (1,)), ((), ())),
        preferred_element_type=jnp.float32,
    )
    dots = dots.reshape(ROT, classes, dots.shape[1])
    noise = jnp.concatenate([near_info[0:1, :], far_info[0:1, :]], axis=1)
    return noise[None] * (dots - 0.5 * energy[None])


def early_kernel(refs_ref, own_ref, far_ref, near_info, far_info, logits_ref, turned_ref):
    logits_ref[...] = score(refs_ref, own_ref, far_ref, near_info, far_info, turned_ref)


def late_kernel(refs_ref, own_ref, far_ref, near_info, far_info, early_ref, logits_ref, part_ref, turned_ref):
    late = score(refs_ref, own_ref, far_ref, near_info, far_info, turned_ref)
    logits_ref[...] = late
    early = early_ref[...]
    top = jnp.maximum(jnp.max(late, axis=0), jnp.max(early, axis=0))
    top = jnp.max(top, axis=0, keepdims=True)
    total = jnp.sum(jnp.exp(late - top[None]), axis=0) + jnp.sum(jnp.exp(early - top[None]), axis=0)
    part_ref[...] = top + jnp.log(jnp.sum(total, axis=0, keepdims=True))


def back_kernel(bits, owned, first, logits_ref, near_ref, other_ref, own_ref, far_ref, near_info, far_info,
                sums_ref, log_ref=None):
    classes, rows = logits_ref.shape[1:]
    here = own_ref.shape[0]
    me = lax.axis_index("blk")
    near = near_ref[...]
    far = jnp.concatenate([other_ref[:, here:], other_ref[:, :here]], axis=1)
    top = jnp.maximum(near, far)
    log_evidence = top + jnp.log(jnp.exp(near - top) + jnp.exp(far - top))
    if log_ref is not None:
        log_ref[...] = log_evidence[:, :log_ref.shape[1]]

    row = lax.broadcasted_iota(jnp.int32, (classes, rows), 0) + first
    place = row // owned
    mixed = jnp.zeros_like(place)
    for i in range(bits - 1):
        mixed = mixed + (((place >> i) & 1) << (bits - 1 - i))
    ident = (mixed ^ me) * owned + row % owned
    names = jnp.concatenate([near_info[...], far_info[...]], axis=1).astype(jnp.int32)
    named = ident == names[1:2, :]
    for j in range(1, TOPK):
        named = named | (ident == names[1 + j:2 + j, :])
    post = jnp.where(named[None], jnp.exp(logits_ref[...] - log_evidence[None]), 0.0)
    weights = jnp.sum(post, axis=0).astype(jnp.bfloat16).astype(jnp.float32)
    mass = jnp.broadcast_to(jnp.sum(weights, axis=1, keepdims=True), (classes, LANES))
    sums_ref[:, WIDTH:] = mass.astype(sums_ref.dtype)

    count = ROT * classes
    post = post.reshape(count, rows)
    high = post.astype(jnp.bfloat16)
    low = (post - high.astype(jnp.float32)).astype(jnp.bfloat16)
    both = jnp.concatenate([high, low], axis=0)
    group = FINE * classes
    for c in range(0, CYCLES, 2):
        chunk = particles_of(own_ref, far_ref, c * ANGLES, 2 * ANGLES)
        part = jnp.dot(both, chunk, preferred_element_type=jnp.float32)
        part = part[:count] + part[count:]
        for d in range(2):
            blocks = []
            for v in range(COARSE):
                block = None
                for q in range(COARSE):
                    at = d * ANGLES + (v + q) % COARSE * LANES
                    piece = part[q * group:(q + 1) * group, at:at + LANES]
                    block = piece if block is None else block + piece
                blocks.append(block)
            turned = jnp.concatenate(blocks, axis=1)
            summed = turned[(FINE - 1) * classes:]
            for s in range(FINE - 2, -1, -1):
                summed = turned[s * classes:(s + 1) * classes] + pltpu.roll(summed, ANGLES - STEP, 1)
            sums_ref[:, (c + d) * ANGLES:(c + d + 1) * ANGLES] = summed.astype(sums_ref.dtype)


def last_kernel(keep_ref, got_ref, sums_ref, mass_ref):
    owned = sums_ref.shape[0]
    total = keep_ref[0:owned, :] + got_ref[...].astype(jnp.float32)
    sums_ref[...] = total[:, :WIDTH]
    for i in range(owned):
        mass_ref[i] = total[i, WIDTH]


def local(particles, references, inv_noise, assign):
    rows, width = particles.shape
    owned = references.shape[0]
    devices = lax.axis_size("blk")
    bits = devices.bit_length() - 1
    half = owned * devices // 4
    both = 2 * rows
    wide = width + LANES
    f32, bf16 = jnp.float32, jnp.bfloat16

    def swap(x, bit):
        return lax.ppermute(x, "blk", [(i, i ^ bit) for i in range(devices)])

    p_far = swap(particles, 1)
    held = [pltpu.with_memory_space_constraint(x, pltpu.HBM)
            for x in (references, particles, inv_noise[None, :], assign.T)]
    own, p_own, near_info, *_ = pl.pallas_call(
        stage_kernel,
        out_shape=(
            jax.ShapeDtypeStruct((owned, width), bf16),
            jax.ShapeDtypeStruct((rows, width), bf16),
            jax.ShapeDtypeStruct((1 + TOPK, rows), f32),
            jax.ShapeDtypeStruct((1, rows), f32),
            jax.ShapeDtypeStruct((TOPK, rows), jnp.int32),
        ),
        in_specs=[HBM] * 4, out_specs=[VMEM] * 5,
        scratch_shapes=[pltpu.SemaphoreType.DMA((4,))],
        compiler_params=PARAMS, name="stage",
    )(*held)
    far_info = swap(near_info, 1)

    gathered = references
    for b in range(bits - 1, 0, -1):
        got = swap(gathered, 1 << b)
        if b == bits - 1:
            gathered = own
        if b > 1:
            gathered = jnp.concatenate([gathered, got], axis=0)

    turned = pltpu.VMEM((ROT * half, width), bf16)
    cost = pl.CostEstimate(
        flops=2 * ROT * half * both * width, bytes_accessed=4 * both * width, transcendentals=0)
    shared = (p_own, p_far, near_info, far_info)
    early = pl.pallas_call(
        early_kernel,
        out_shape=jax.ShapeDtypeStruct((ROT, half, both), f32),
        in_specs=[VMEM] * 5, out_specs=VMEM, scratch_shapes=[turned],
        compiler_params=PARAMS, cost_estimate=cost, name="early",
    )(gathered, *shared)
    late, near = pl.pallas_call(
        late_kernel,
        out_shape=(jax.ShapeDtypeStruct((ROT, half, both), f32), jax.ShapeDtypeStruct((1, both), f32)),
        in_specs=[VMEM] * 6, out_specs=[VMEM] * 2, scratch_shapes=[turned],
        compiler_params=PARAMS, cost_estimate=cost, name="late",
    )(got, *shared, early)
    other = swap(near, 1)

    send = pl.pallas_call(
        functools.partial(back_kernel, bits, owned, half),
        out_shape=jax.ShapeDtypeStruct((half, wide), bf16),
        in_specs=[VMEM] * 7, out_specs=VMEM,
        compiler_params=PARAMS, cost_estimate=cost, name="back_send",
    )(late, near, other, *shared)
    keep, log_evidence = pl.pallas_call(
        functools.partial(back_kernel, bits, owned, 0),
        out_shape=(jax.ShapeDtypeStruct((half, wide), f32), jax.ShapeDtypeStruct((1, rows), f32)),
        in_specs=[VMEM] * 7, out_specs=[VMEM] * 2,
        compiler_params=PARAMS, cost_estimate=cost, name="back_keep",
    )(early, near, other, *shared)

    for b in range(1, bits):
        got = swap(send, 1 << b)
        if b < bits - 1:
            total = keep + got.astype(f32)
            part = total.shape[0] // 2
            keep, send = total[:part], total[part:].astype(bf16)
    sums, mass = pl.pallas_call(
        last_kernel,
        out_shape=(jax.ShapeDtypeStruct((owned, width), f32), jax.ShapeDtypeStruct((owned,), f32)),
        in_specs=[VMEM] * 2,
        out_specs=[VMEM, pl.BlockSpec(memory_space=pltpu.SMEM)],
        compiler_params=PARAMS, name="last",
    )(keep, got)
    return sums, mass, log_evidence[0]


def solution(mesh):
    placed = (
        P(("parts", "blk"), None),
        P(("parts", "blk"), None),
        P(("parts", "blk")),
        P(("parts", "blk"), None),
    )
    return jax.shard_map(
        local,
        mesh=mesh,
        in_specs=placed,
        out_specs=(P(("parts", "blk"), None), P(("parts", "blk")), P(("parts", "blk"))),
        check_vma=False,
    )
```

```python
import functools

import jax
import jax.numpy as jnp
from jax import lax
from jax.experimental import pallas as pl
from jax.experimental.pallas import tpu as pltpu
from jax.sharding import PartitionSpec as P

ROT = 12
CYCLES = 12
ANGLES = 384
TOPK = 2
WIDTH = CYCLES * ANGLES
LANES = 128
STEP = ANGLES // ROT
FINE = LANES // STEP
COARSE = ROT // FINE
VMEM = pl.BlockSpec(memory_space=pltpu.VMEM)
HBM = pl.BlockSpec(memory_space=pltpu.HBM)
PARAMS = pltpu.CompilerParams(vmem_limit_bytes=40 * 1024 * 1024)


def stage_kernel(refs, noise, names, particles, refs_ref, packed_ref, p_ref, noise_ref, names_ref, sems):
    copies = [
        pltpu.make_async_copy(src, dst, sems.at[i])
        for i, (src, dst) in enumerate(
            ((refs, refs_ref), (noise, noise_ref), (names, names_ref), (particles, p_ref)))
    ]
    for copy in copies:
        copy.start()
    for copy in copies[:3]:
        copy.wait()
    packed_ref[0:1, :] = noise_ref[...]
    packed_ref[1:1 + TOPK, :] = names_ref[...].astype(jnp.float32)
    copies[3].wait()


def flip(p_ref, flipped_ref):
    for at in range(0, WIDTH, LANES):
        flipped_ref[at:at + LANES, :] = p_ref[:, at:at + LANES].T


def flip_kernel(after_ref, p_ref, flipped_ref):
    flip(p_ref, flipped_ref)


def join_kernel(held_ref, got_ref, *rest):
    out_ref = rest[-1]
    count = held_ref.shape[0]
    out_ref[0:count, :] = held_ref[...]
    out_ref[count:2 * count, :] = got_ref[...]


def particles_of(own_ref, far_ref, start, size):
    return jnp.concatenate([own_ref[:, start:start + size], far_ref[:, start:start + size]], axis=0)


def score(refs_ref, own_flipped, far_flipped, near_info, far_info, turned_ref):
    classes = refs_ref.shape[0]
    group = FINE * classes
    energy = jnp.zeros((classes, LANES), jnp.float32)
    for c in range(CYCLES):
        cube = refs_ref[:, c * ANGLES:(c + 1) * ANGLES].astype(jnp.float32)
        for v in range(COARSE):
            piece = cube[:, v * LANES:(v + 1) * LANES]
            energy = energy + piece * piece
        moved = [cube] + [pltpu.roll(cube, s * STEP, 1) for s in range(1, FINE)]
        moved = jnp.concatenate(moved, axis=0).astype(jnp.bfloat16)
        for q in range(COARSE):
            for v in range(COARSE):
                at = c * ANGLES + (v + q) % COARSE * LANES
                turned_ref[q * group:(q + 1) * group, at:at + LANES] = moved[:, v * LANES:(v + 1) * LANES]
    energy = jnp.sum(energy, axis=1, keepdims=True)
    dots = lax.dot_general(
        turned_ref[...], jnp.concatenate([own_flipped[...], far_flipped[...]], axis=1),
        (((1,), (0,)), ((), ())), preferred_element_type=jnp.float32,
    )
    dots = dots.reshape(ROT, classes, dots.shape[1])
    noise = jnp.concatenate([near_info[0:1, :], far_info[0:1, :]], axis=1)
    return noise[None] * (dots - 0.5 * energy[None])


def early_kernel(refs_ref, own_flipped, far_ref, near_info, far_info, logits_ref, far_flipped, turned_ref):
    flip(far_ref, far_flipped)
    logits_ref[...] = score(refs_ref, own_flipped, far_flipped, near_info, far_info, turned_ref)


def late_kernel(refs_ref, own_flipped, far_flipped, near_info, far_info, early_ref, logits_ref, part_ref, turned_ref):
    late = score(refs_ref, own_flipped, far_flipped, near_info, far_info, turned_ref)
    logits_ref[...] = late
    early = early_ref[...]
    top = jnp.maximum(jnp.max(late, axis=0), jnp.max(early, axis=0))
    top = jnp.max(top, axis=0, keepdims=True)
    total = jnp.sum(jnp.exp(late - top[None]), axis=0) + jnp.sum(jnp.exp(early - top[None]), axis=0)
    part_ref[...] = top + jnp.log(jnp.sum(total, axis=0, keepdims=True))


def back_kernel(bits, owned, first, logits_ref, near_ref, other_ref, own_ref, far_ref, near_info, far_info,
                sums_ref, log_ref=None):
    classes, rows = logits_ref.shape[1:]
    here = own_ref.shape[0]
    me = lax.axis_index("blk")
    near = near_ref[...]
    far = jnp.concatenate([other_ref[:, here:], other_ref[:, :here]], axis=1)
    top = jnp.maximum(near, far)
    log_evidence = top + jnp.log(jnp.exp(near - top) + jnp.exp(far - top))
    if log_ref is not None:
        log_ref[...] = log_evidence[:, :log_ref.shape[1]]

    row = lax.broadcasted_iota(jnp.int32, (classes, rows), 0) + first
    place = row // owned
    mixed = jnp.zeros_like(place)
    color = me
    for i in range(1, bits):
        color = color ^ (me >> i)
    for i, (even, odd) in enumerate(offsets(bits)):
        mixed = mixed ^ ((place >> i) & 1) * jnp.where(color % 2 == 0, even, odd)
    ident = (mixed ^ me) * owned + row % owned
    names = jnp.concatenate([near_info[...], far_info[...]], axis=1).astype(jnp.int32)
    named = ident == names[1:2, :]
    for j in range(1, TOPK):
        named = named | (ident == names[1 + j:2 + j, :])
    post = jnp.where(named[None], jnp.exp(logits_ref[...] - log_evidence[None]), 0.0)
    weights = jnp.sum(post, axis=0).astype(jnp.bfloat16).astype(jnp.float32)
    mass = jnp.broadcast_to(jnp.sum(weights, axis=1, keepdims=True), (classes, LANES))
    sums_ref[:, WIDTH:] = mass.astype(sums_ref.dtype)

    count = ROT * classes
    post = post.reshape(count, rows)
    high = post.astype(jnp.bfloat16)
    low = (post - high.astype(jnp.float32)).astype(jnp.bfloat16)
    both = jnp.concatenate([high, low], axis=0)
    group = FINE * classes
    for c in range(0, CYCLES, 2):
        chunk = particles_of(own_ref, far_ref, c * ANGLES, 2 * ANGLES)
        part = jnp.dot(both, chunk, preferred_element_type=jnp.float32)
        part = part[:count] + part[count:]
        for d in range(2):
            blocks = []
            for v in range(COARSE):
                block = None
                for q in range(COARSE):
                    at = d * ANGLES + (v + q) % COARSE * LANES
                    piece = part[q * group:(q + 1) * group, at:at + LANES]
                    block = piece if block is None else block + piece
                blocks.append(block)
            turned = jnp.concatenate(blocks, axis=1)
            summed = turned[(FINE - 1) * classes:]
            for s in range(FINE - 2, -1, -1):
                summed = turned[s * classes:(s + 1) * classes] + pltpu.roll(summed, ANGLES - STEP, 1)
            sums_ref[:, (c + d) * ANGLES:(c + d + 1) * ANGLES] = summed.astype(sums_ref.dtype)


def last_kernel(keep_ref, got_ref, sums_ref, mass_ref):
    owned = sums_ref.shape[0]
    total = keep_ref[0:owned, :] + got_ref[...].astype(jnp.float32)
    sums_ref[...] = total[:, :WIDTH]
    for i in range(owned):
        mass_ref[i] = total[i, WIDTH]


def offsets(bits):
    even = [(1 << b) | 1 for b in range(bits - 1, 0, -1)]
    odd = even[:-2] + even[:-3:-1]
    return list(zip(even, odd))


def local(particles, references, inv_noise, assign):
    rows, width = particles.shape
    owned = references.shape[0]
    devices = lax.axis_size("blk")
    bits = devices.bit_length() - 1
    half = owned * devices // 4
    both = 2 * rows
    wide = width + LANES
    f32, bf16 = jnp.float32, jnp.bfloat16

    def swap(x, even, odd):
        return lax.ppermute(x, "blk", [(i, i ^ (odd if i.bit_count() % 2 else even)) for i in range(devices)])

    def join(*operands):
        held = operands[0]
        return pl.pallas_call(
            join_kernel, out_shape=jax.ShapeDtypeStruct((2 * held.shape[0], width), bf16),
            in_specs=[VMEM] * len(operands), out_specs=VMEM, compiler_params=PARAMS, name="join",
        )(*operands)

    rounds = offsets(bits)
    got = swap(references, *rounds[0])
    p_far = swap(particles, 1, 1)
    held = [pltpu.with_memory_space_constraint(x, pltpu.HBM)
            for x in (references, inv_noise[None, :], assign.T, particles)]
    own, near_info, p_own = pl.pallas_call(
        stage_kernel,
        out_shape=(
            jax.ShapeDtypeStruct((owned, width), bf16),
            jax.ShapeDtypeStruct((1 + TOPK, rows), f32),
            jax.ShapeDtypeStruct((rows, width), bf16),
        ),
        in_specs=[HBM] * 4, out_specs=[VMEM] * 3,
        scratch_shapes=[
            pltpu.VMEM((1, rows), f32), pltpu.VMEM((TOPK, rows), jnp.int32), pltpu.SemaphoreType.DMA((4,))],
        compiler_params=PARAMS, name="stage",
    )(*held)
    far_info = swap(near_info, 1, 1)

    gathered = join(own, got)
    own_flipped = pl.pallas_call(
        flip_kernel, out_shape=jax.ShapeDtypeStruct((width, rows), bf16),
        in_specs=[VMEM] * 2, out_specs=VMEM, compiler_params=PARAMS, name="flip",
    )(gathered, p_own)
    for r, pair in enumerate(rounds[1:], 1):
        got = swap(gathered, *pair)
        if r < len(rounds) - 1:
            gathered = join(gathered, got, own_flipped, far_info)

    turned = pltpu.VMEM((ROT * half, width), bf16)
    cost = pl.CostEstimate(
        flops=2 * ROT * half * both * width, bytes_accessed=4 * both * width, transcendentals=0)
    info = (near_info, far_info)
    early, far_flipped = pl.pallas_call(
        early_kernel,
        out_shape=(jax.ShapeDtypeStruct((ROT, half, both), f32), jax.ShapeDtypeStruct((width, rows), bf16)),
        in_specs=[VMEM] * 5, out_specs=[VMEM] * 2, scratch_shapes=[turned],
        compiler_params=PARAMS, cost_estimate=cost, name="early",
    )(gathered, own_flipped, p_far, *info)
    late, near = pl.pallas_call(
        late_kernel,
        out_shape=(jax.ShapeDtypeStruct((ROT, half, both), f32), jax.ShapeDtypeStruct((1, both), f32)),
        in_specs=[VMEM] * 6, out_specs=[VMEM] * 2, scratch_shapes=[turned],
        compiler_params=PARAMS, cost_estimate=cost, name="late",
    )(got, own_flipped, far_flipped, *info, early)
    other = swap(near, 1, 1)
    shared = (p_own, p_far, *info)

    send = pl.pallas_call(
        functools.partial(back_kernel, bits, owned, half),
        out_shape=jax.ShapeDtypeStruct((half, wide), bf16),
        in_specs=[VMEM] * 7, out_specs=VMEM,
        compiler_params=PARAMS, cost_estimate=cost, name="back_send",
    )(late, near, other, *shared)
    keep, log_evidence = pl.pallas_call(
        functools.partial(back_kernel, bits, owned, 0),
        out_shape=(jax.ShapeDtypeStruct((half, wide), f32), jax.ShapeDtypeStruct((1, rows), f32)),
        in_specs=[VMEM] * 7, out_specs=[VMEM] * 2,
        compiler_params=PARAMS, cost_estimate=cost, name="back_keep",
    )(early, near, other, *shared)

    for r, pair in enumerate(rounds[::-1], 1):
        got = swap(send, *pair)
        if r < len(rounds):
            total = keep + got.astype(f32)
            part = total.shape[0] // 2
            keep, send = total[:part], total[part:].astype(bf16)
    sums, mass = pl.pallas_call(
        last_kernel,
        out_shape=(jax.ShapeDtypeStruct((owned, width), f32), jax.ShapeDtypeStruct((owned,), f32)),
        in_specs=[VMEM] * 2,
        out_specs=[VMEM, pl.BlockSpec(memory_space=pltpu.SMEM)],
        compiler_params=PARAMS, name="last",
    )(keep, got)
    return sums, mass, log_evidence[0]


def solution(mesh):
    placed = (
        P(("parts", "blk"), None),
        P(("parts", "blk"), None),
        P(("parts", "blk")),
        P(("parts", "blk"), None),
    )
    return jax.shard_map(
        local,
        mesh=mesh,
        in_specs=placed,
        out_specs=(P(("parts", "blk"), None), P(("parts", "blk")), P(("parts", "blk"))),
        check_vma=False,
    )
```

```python
import functools

import jax
import jax.numpy as jnp
from jax import lax
from jax.experimental import pallas as pl
from jax.experimental.pallas import tpu as pltpu
from jax.sharding import PartitionSpec as P

ROT = 12
CYCLES = 12
ANGLES = 384
TOPK = 2
FLIPS = 4
WIDTH = CYCLES * ANGLES
LANES = 128
STEP = ANGLES // ROT
FINE = LANES // STEP
COARSE = ROT // FINE
VMEM = pl.BlockSpec(memory_space=pltpu.VMEM)
HBM = pl.BlockSpec(memory_space=pltpu.HBM)
PARAMS = pltpu.CompilerParams(vmem_limit_bytes=40 * 1024 * 1024)


def stage_kernel(refs, noise, names, refs_ref, packed_ref, noise_ref, names_ref, sems):
    copies = [
        pltpu.make_async_copy(src, dst, sems.at[i])
        for i, (src, dst) in enumerate(((refs, refs_ref), (noise, noise_ref), (names, names_ref)))
    ]
    for copy in copies:
        copy.start()
    for copy in copies:
        copy.wait()
    packed_ref[0:1, :] = noise_ref[...]
    packed_ref[1:1 + TOPK, :] = names_ref[...].astype(jnp.float32)


def flip(p_ref, flipped_ref, start, stop):
    for at in range(start, stop, LANES):
        flipped_ref[at:at + LANES, :] = p_ref[:, at:at + LANES].T


def flip_kernel(after_ref, particles, p_ref, flipped_ref, sems):
    part = WIDTH // FLIPS
    copies = [
        pltpu.make_async_copy(
            particles.at[:, i * part:(i + 1) * part], p_ref.at[:, i * part:(i + 1) * part], sems.at[i])
        for i in range(FLIPS)
    ]
    for copy in copies:
        copy.start()
    for i, copy in enumerate(copies):
        copy.wait()
        flip(p_ref, flipped_ref, i * part, (i + 1) * part)


def join_kernel(held_ref, got_ref, *rest):
    out_ref = rest[-1]
    count = held_ref.shape[0]
    out_ref[0:count, :] = held_ref[...]
    out_ref[count:2 * count, :] = got_ref[...]


def particles_of(own_ref, far_ref, start, size):
    return jnp.concatenate([own_ref[:, start:start + size], far_ref[:, start:start + size]], axis=0)


def score(refs_ref, own_flipped, far_flipped, near_info, far_info, turned_ref):
    classes = refs_ref.shape[0]
    group = FINE * classes
    energy = jnp.zeros((classes, LANES), jnp.float32)
    for c in range(CYCLES):
        cube = refs_ref[:, c * ANGLES:(c + 1) * ANGLES].astype(jnp.float32)
        for v in range(COARSE):
            piece = cube[:, v * LANES:(v + 1) * LANES]
            energy = energy + piece * piece
        moved = [cube] + [pltpu.roll(cube, s * STEP, 1) for s in range(1, FINE)]
        moved = jnp.concatenate(moved, axis=0).astype(jnp.bfloat16)
        for q in range(COARSE):
            for v in range(COARSE):
                at = c * ANGLES + (v + q) % COARSE * LANES
                turned_ref[q * group:(q + 1) * group, at:at + LANES] = moved[:, v * LANES:(v + 1) * LANES]
    energy = jnp.sum(energy, axis=1, keepdims=True)
    dots = lax.dot_general(
        turned_ref[...], jnp.concatenate([own_flipped[...], far_flipped[...]], axis=1),
        (((1,), (0,)), ((), ())), preferred_element_type=jnp.float32,
    )
    dots = dots.reshape(ROT, classes, dots.shape[1])
    noise = jnp.concatenate([near_info[0:1, :], far_info[0:1, :]], axis=1)
    return noise[None] * (dots - 0.5 * energy[None])


def early_kernel(refs_ref, own_flipped, far_ref, near_info, far_info, logits_ref, far_flipped, turned_ref):
    flip(far_ref, far_flipped, 0, WIDTH)
    logits_ref[...] = score(refs_ref, own_flipped, far_flipped, near_info, far_info, turned_ref)


def late_kernel(refs_ref, own_flipped, far_flipped, near_info, far_info, early_ref, logits_ref, part_ref, turned_ref):
    late = score(refs_ref, own_flipped, far_flipped, near_info, far_info, turned_ref)
    logits_ref[...] = late
    early = early_ref[...]
    top = jnp.maximum(jnp.max(late, axis=0), jnp.max(early, axis=0))
    top = jnp.max(top, axis=0, keepdims=True)
    total = jnp.sum(jnp.exp(late - top[None]), axis=0) + jnp.sum(jnp.exp(early - top[None]), axis=0)
    part_ref[...] = top + jnp.log(jnp.sum(total, axis=0, keepdims=True))


def back_kernel(bits, owned, first, logits_ref, near_ref, other_ref, own_ref, far_ref, near_info, far_info,
                sums_ref, log_ref=None):
    classes, rows = logits_ref.shape[1:]
    here = own_ref.shape[0]
    me = lax.axis_index("blk")
    near = near_ref[...]
    far = jnp.concatenate([other_ref[:, here:], other_ref[:, :here]], axis=1)
    top = jnp.maximum(near, far)
    log_evidence = top + jnp.log(jnp.exp(near - top) + jnp.exp(far - top))
    if log_ref is not None:
        log_ref[...] = log_evidence[:, :log_ref.shape[1]]

    row = lax.broadcasted_iota(jnp.int32, (classes, rows), 0) + first
    place = row // owned
    mixed = jnp.zeros_like(place)
    color = me
    for i in range(1, bits):
        color = color ^ (me >> i)
    for i, (even, odd) in enumerate(offsets(bits)):
        mixed = mixed ^ ((place >> i) & 1) * jnp.where(color % 2 == 0, even, odd)
    ident = (mixed ^ me) * owned + row % owned
    names = jnp.concatenate([near_info[...], far_info[...]], axis=1).astype(jnp.int32)
    named = ident == names[1:2, :]
    for j in range(1, TOPK):
        named = named | (ident == names[1 + j:2 + j, :])
    post = jnp.where(named[None], jnp.exp(logits_ref[...] - log_evidence[None]), 0.0)
    weights = jnp.sum(post, axis=0).astype(jnp.bfloat16).astype(jnp.float32)
    mass = jnp.broadcast_to(jnp.sum(weights, axis=1, keepdims=True), (classes, LANES))
    sums_ref[:, WIDTH:] = mass.astype(sums_ref.dtype)

    count = ROT * classes
    post = post.reshape(count, rows)
    high = post.astype(jnp.bfloat16)
    low = (post - high.astype(jnp.float32)).astype(jnp.bfloat16)
    both = jnp.concatenate([high, low], axis=0)
    group = FINE * classes
    for c in range(0, CYCLES, 2):
        chunk = particles_of(own_ref, far_ref, c * ANGLES, 2 * ANGLES)
        part = jnp.dot(both, chunk, preferred_element_type=jnp.float32)
        part = part[:count] + part[count:]
        for d in range(2):
            blocks = []
            for v in range(COARSE):
                block = None
                for q in range(COARSE):
                    at = d * ANGLES + (v + q) % COARSE * LANES
                    piece = part[q * group:(q + 1) * group, at:at + LANES]
                    block = piece if block is None else block + piece
                blocks.append(block)
            turned = jnp.concatenate(blocks, axis=1)
            summed = turned[(FINE - 1) * classes:]
            for s in range(FINE - 2, -1, -1):
                summed = turned[s * classes:(s + 1) * classes] + pltpu.roll(summed, ANGLES - STEP, 1)
            sums_ref[:, (c + d) * ANGLES:(c + d + 1) * ANGLES] = summed.astype(sums_ref.dtype)


def last_kernel(keep_ref, got_ref, sums_ref, mass_ref):
    owned = sums_ref.shape[0]
    total = keep_ref[0:owned, :] + got_ref[...].astype(jnp.float32)
    sums_ref[...] = total[:, :WIDTH]
    for i in range(owned):
        mass_ref[i] = total[i, WIDTH]


def offsets(bits):
    even = [(1 << b) | 1 for b in range(bits - 1, 0, -1)]
    odd = even[:-2] + even[:-3:-1]
    return list(zip(even, odd))


def local(particles, references, inv_noise, assign):
    rows, width = particles.shape
    owned = references.shape[0]
    devices = lax.axis_size("blk")
    bits = devices.bit_length() - 1
    half = owned * devices // 4
    both = 2 * rows
    wide = width + LANES
    f32, bf16 = jnp.float32, jnp.bfloat16

    def swap(x, even, odd):
        return lax.ppermute(x, "blk", [(i, i ^ (odd if i.bit_count() % 2 else even)) for i in range(devices)])

    def join(*operands):
        held = operands[0]
        return pl.pallas_call(
            join_kernel, out_shape=jax.ShapeDtypeStruct((2 * held.shape[0], width), bf16),
            in_specs=[VMEM] * len(operands), out_specs=VMEM, compiler_params=PARAMS, cost_estimate=pl.CostEstimate(flops=4000000000, bytes_accessed=12000000, transcendentals=0), name="join",
        )(*operands)

    rounds = offsets(bits)
    p_far = swap(particles, 1, 1)
    held = [pltpu.with_memory_space_constraint(x, pltpu.HBM)
            for x in (references, inv_noise[None, :], assign.T, particles)]
    own, near_info = pl.pallas_call(
        stage_kernel,
        out_shape=(jax.ShapeDtypeStruct((owned, width), bf16), jax.ShapeDtypeStruct((1 + TOPK, rows), f32)),
        in_specs=[HBM] * 3, out_specs=[VMEM] * 2,
        scratch_shapes=[
            pltpu.VMEM((1, rows), f32), pltpu.VMEM((TOPK, rows), jnp.int32), pltpu.SemaphoreType.DMA((3,))],
        compiler_params=PARAMS, cost_estimate=pl.CostEstimate(flops=4000000000, bytes_accessed=12000000, transcendentals=0), name="stage",
    )(*held[:3])
    far_info = swap(near_info, 1, 1)

    got = swap(references, *rounds[0])
    gathered = join(own, got)
    p_own, own_flipped = pl.pallas_call(
        flip_kernel,
        out_shape=(jax.ShapeDtypeStruct((rows, width), bf16), jax.ShapeDtypeStruct((width, rows), bf16)),
        in_specs=[VMEM, HBM], out_specs=[VMEM] * 2, scratch_shapes=[pltpu.SemaphoreType.DMA((FLIPS,))],
        compiler_params=PARAMS, cost_estimate=pl.CostEstimate(flops=4000000000, bytes_accessed=12000000, transcendentals=0), name="flip",
    )(gathered, held[3])
    for r, pair in enumerate(rounds[1:], 1):
        got = swap(gathered, *pair)
        if r < len(rounds) - 1:
            gathered = join(gathered, got, own_flipped, far_info)

    turned = pltpu.VMEM((ROT * half, width), bf16)
    cost = pl.CostEstimate(
        flops=2 * ROT * half * both * width, bytes_accessed=4 * both * width, transcendentals=0)
    info = (near_info, far_info)
    early, far_flipped = pl.pallas_call(
        early_kernel,
        out_shape=(jax.ShapeDtypeStruct((ROT, half, both), f32), jax.ShapeDtypeStruct((width, rows), bf16)),
        in_specs=[VMEM] * 5, out_specs=[VMEM] * 2, scratch_shapes=[turned],
        compiler_params=PARAMS, cost_estimate=cost, name="early",
    )(gathered, own_flipped, p_far, *info)
    late, near = pl.pallas_call(
        late_kernel,
        out_shape=(jax.ShapeDtypeStruct((ROT, half, both), f32), jax.ShapeDtypeStruct((1, both), f32)),
        in_specs=[VMEM] * 6, out_specs=[VMEM] * 2, scratch_shapes=[turned],
        compiler_params=PARAMS, cost_estimate=cost, name="late",
    )(got, own_flipped, far_flipped, *info, early)
    other = swap(near, 1, 1)
    shared = (p_own, p_far, *info)

    send = pl.pallas_call(
        functools.partial(back_kernel, bits, owned, half),
        out_shape=jax.ShapeDtypeStruct((half, wide), bf16),
        in_specs=[VMEM] * 7, out_specs=VMEM,
        compiler_params=PARAMS, cost_estimate=cost, name="back_send",
    )(late, near, other, *shared)
    keep, log_evidence = pl.pallas_call(
        functools.partial(back_kernel, bits, owned, 0),
        out_shape=(jax.ShapeDtypeStruct((half, wide), f32), jax.ShapeDtypeStruct((1, rows), f32)),
        in_specs=[VMEM] * 7, out_specs=[VMEM] * 2,
        compiler_params=PARAMS, cost_estimate=cost, name="back_keep",
    )(early, near, other, *shared)

    for r, pair in enumerate(rounds[::-1], 1):
        got = swap(send, *pair)
        if r < len(rounds):
            total = keep + got.astype(f32)
            part = total.shape[0] // 2
            keep, send = total[:part], total[part:].astype(bf16)
    sums, mass = pl.pallas_call(
        last_kernel,
        out_shape=(jax.ShapeDtypeStruct((owned, width), f32), jax.ShapeDtypeStruct((owned,), f32)),
        in_specs=[VMEM] * 2,
        out_specs=[VMEM, pl.BlockSpec(memory_space=pltpu.SMEM)],
        compiler_params=PARAMS, name="last",
    )(keep, got)
    return sums, mass, log_evidence[0]


def solution(mesh):
    placed = (
        P(("parts", "blk"), None),
        P(("parts", "blk"), None),
        P(("parts", "blk")),
        P(("parts", "blk"), None),
    )
    return jax.shard_map(
        local,
        mesh=mesh,
        in_specs=placed,
        out_specs=(P(("parts", "blk"), None), P(("parts", "blk")), P(("parts", "blk"))),
        check_vma=False,
    )
```

```python
import functools

import jax
import jax.numpy as jnp
from jax import lax
from jax.experimental import pallas as pl
from jax.experimental.pallas import tpu as pltpu
from jax.sharding import PartitionSpec as P

ROT = 12
CYCLES = 12
ANGLES = 384
TOPK = 2
FLIPS = 4
WIDTH = CYCLES * ANGLES
LANES = 128
STEP = ANGLES // ROT
FINE = LANES // STEP
COARSE = ROT // FINE
VMEM = pl.BlockSpec(memory_space=pltpu.VMEM)
HBM = pl.BlockSpec(memory_space=pltpu.HBM)
PARAMS = pltpu.CompilerParams(vmem_limit_bytes=40 * 1024 * 1024)


def stage_kernel(refs, noise, names, refs_ref, packed_ref, noise_ref, names_ref, sems):
    copies = [
        pltpu.make_async_copy(src, dst, sems.at[i])
        for i, (src, dst) in enumerate(((refs, refs_ref), (noise, noise_ref), (names, names_ref)))
    ]
    for copy in copies:
        copy.start()
    for copy in copies:
        copy.wait()
    packed_ref[0:1, :] = noise_ref[...]
    packed_ref[1:1 + TOPK, :] = names_ref[...].astype(jnp.float32)


def flip(p_ref, flipped_ref, start, stop):
    for at in range(start, stop, LANES):
        flipped_ref[at:at + LANES, :] = p_ref[:, at:at + LANES].T


def flip_kernel(after_ref, particles, p_ref, flipped_ref, sems):
    part = WIDTH // FLIPS
    copies = [
        pltpu.make_async_copy(
            particles.at[:, i * part:(i + 1) * part], p_ref.at[:, i * part:(i + 1) * part], sems.at[i])
        for i in range(FLIPS)
    ]
    for copy in copies:
        copy.start()
    for i, copy in enumerate(copies):
        copy.wait()
        flip(p_ref, flipped_ref, i * part, (i + 1) * part)


def join_kernel(held_ref, got_ref, *rest):
    out_ref = rest[-1]
    count = held_ref.shape[0]
    out_ref[0:count, :] = held_ref[...]
    out_ref[count:2 * count, :] = got_ref[...]


def particles_of(own_ref, far_ref, start, size):
    return jnp.concatenate([own_ref[:, start:start + size], far_ref[:, start:start + size]], axis=0)


def score(refs_ref, own_flipped, far_flipped, near_info, far_info, turned_ref):
    classes = refs_ref.shape[0]
    group = FINE * classes
    energy = jnp.zeros((classes, LANES), jnp.float32)
    for c in range(CYCLES):
        cube = refs_ref[:, c * ANGLES:(c + 1) * ANGLES].astype(jnp.float32)
        for v in range(COARSE):
            piece = cube[:, v * LANES:(v + 1) * LANES]
            energy = energy + piece * piece
        moved = [cube] + [pltpu.roll(cube, s * STEP, 1) for s in range(1, FINE)]
        moved = jnp.concatenate(moved, axis=0).astype(jnp.bfloat16)
        for q in range(COARSE):
            for v in range(COARSE):
                at = c * ANGLES + (v + q) % COARSE * LANES
                turned_ref[q * group:(q + 1) * group, at:at + LANES] = moved[:, v * LANES:(v + 1) * LANES]
    energy = jnp.sum(energy, axis=1, keepdims=True)
    dots = lax.dot_general(
        turned_ref[...], jnp.concatenate([own_flipped[...], far_flipped[...]], axis=1),
        (((1,), (0,)), ((), ())), preferred_element_type=jnp.float32,
    )
    dots = dots.reshape(ROT, classes, dots.shape[1])
    noise = jnp.concatenate([near_info[0:1, :], far_info[0:1, :]], axis=1)
    return noise[None] * (dots - 0.5 * energy[None])


def early_kernel(refs_ref, own_flipped, far_ref, near_info, far_info, logits_ref, far_flipped, turned_ref):
    flip(far_ref, far_flipped, 0, WIDTH)
    logits_ref[...] = score(refs_ref, own_flipped, far_flipped, near_info, far_info, turned_ref)


def late_kernel(refs_ref, own_flipped, far_flipped, near_info, far_info, early_ref, logits_ref, part_ref, turned_ref):
    late = score(refs_ref, own_flipped, far_flipped, near_info, far_info, turned_ref)
    logits_ref[...] = late
    early = early_ref[...]
    top = jnp.maximum(jnp.max(late, axis=0), jnp.max(early, axis=0))
    top = jnp.max(top, axis=0, keepdims=True)
    total = jnp.sum(jnp.exp(late - top[None]), axis=0) + jnp.sum(jnp.exp(early - top[None]), axis=0)
    part_ref[...] = top + jnp.log(jnp.sum(total, axis=0, keepdims=True))


def back_kernel(bits, owned, first, logits_ref, near_ref, other_ref, own_ref, far_ref, near_info, far_info,
                sums_ref, log_ref=None):
    classes, rows = logits_ref.shape[1:]
    here = own_ref.shape[0]
    me = lax.axis_index("blk")
    near = near_ref[...]
    far = jnp.concatenate([other_ref[:, here:], other_ref[:, :here]], axis=1)
    top = jnp.maximum(near, far)
    log_evidence = top + jnp.log(jnp.exp(near - top) + jnp.exp(far - top))
    if log_ref is not None:
        log_ref[...] = log_evidence[:, :log_ref.shape[1]]

    row = lax.broadcasted_iota(jnp.int32, (classes, rows), 0) + first
    place = row // owned
    mixed = jnp.zeros_like(place)
    color = me
    for i in range(1, bits):
        color = color ^ (me >> i)
    for i, (even, odd) in enumerate(offsets(bits)):
        mixed = mixed ^ ((place >> i) & 1) * jnp.where(color % 2 == 0, even, odd)
    ident = (mixed ^ me) * owned + row % owned
    names = jnp.concatenate([near_info[...], far_info[...]], axis=1).astype(jnp.int32)
    named = ident == names[1:2, :]
    for j in range(1, TOPK):
        named = named | (ident == names[1 + j:2 + j, :])
    post = jnp.where(named[None], jnp.exp(logits_ref[...] - log_evidence[None]), 0.0)
    weights = jnp.sum(post, axis=0).astype(jnp.bfloat16).astype(jnp.float32)
    mass = jnp.broadcast_to(jnp.sum(weights, axis=1, keepdims=True), (classes, LANES))
    sums_ref[:, WIDTH:] = mass.astype(sums_ref.dtype)

    count = ROT * classes
    post = post.reshape(count, rows)
    high = post.astype(jnp.bfloat16)
    low = (post - high.astype(jnp.float32)).astype(jnp.bfloat16)
    both = jnp.concatenate([high, low], axis=0)
    group = FINE * classes
    for c in range(0, CYCLES, 2):
        chunk = particles_of(own_ref, far_ref, c * ANGLES, 2 * ANGLES)
        part = jnp.dot(both, chunk, preferred_element_type=jnp.float32)
        part = part[:count] + part[count:]
        for d in range(2):
            blocks = []
            for v in range(COARSE):
                block = None
                for q in range(COARSE):
                    at = d * ANGLES + (v + q) % COARSE * LANES
                    piece = part[q * group:(q + 1) * group, at:at + LANES]
                    block = piece if block is None else block + piece
                blocks.append(block)
            turned = jnp.concatenate(blocks, axis=1)
            summed = turned[:classes]
            for s in range(1, FINE):
                summed = summed + pltpu.roll(turned[s * classes:(s + 1) * classes], ANGLES - s * STEP, 1)
            sums_ref[:, (c + d) * ANGLES:(c + d + 1) * ANGLES] = summed.astype(sums_ref.dtype)


def last_kernel(keep_ref, got_ref, sums_ref, mass_ref):
    owned = sums_ref.shape[0]
    total = keep_ref[0:owned, :] + got_ref[...].astype(jnp.float32)
    sums_ref[...] = total[:, :WIDTH]
    for i in range(owned):
        mass_ref[i] = total[i, WIDTH]


def offsets(bits):
    even = [(1 << b) | 1 for b in range(bits - 1, 0, -1)]
    odd = even[:-2] + even[:-3:-1]
    return list(zip(even, odd))


def local(particles, references, inv_noise, assign):
    rows, width = particles.shape
    owned = references.shape[0]
    devices = lax.axis_size("blk")
    bits = devices.bit_length() - 1
    half = owned * devices // 4
    both = 2 * rows
    wide = width + LANES
    f32, bf16 = jnp.float32, jnp.bfloat16

    def swap(x, even, odd):
        return lax.ppermute(x, "blk", [(i, i ^ (odd if i.bit_count() % 2 else even)) for i in range(devices)])

    def join(*operands):
        held = operands[0]
        return pl.pallas_call(
            join_kernel, out_shape=jax.ShapeDtypeStruct((2 * held.shape[0], width), bf16),
            in_specs=[VMEM] * len(operands), out_specs=VMEM, compiler_params=PARAMS, cost_estimate=pl.CostEstimate(flops=4000000000, bytes_accessed=12000000, transcendentals=0), name="join",
        )(*operands)

    rounds = offsets(bits)
    p_far = swap(particles, 1, 1)
    held = [pltpu.with_memory_space_constraint(x, pltpu.HBM)
            for x in (references, inv_noise[None, :], assign.T, particles)]
    own, near_info = pl.pallas_call(
        stage_kernel,
        out_shape=(jax.ShapeDtypeStruct((owned, width), bf16), jax.ShapeDtypeStruct((1 + TOPK, rows), f32)),
        in_specs=[HBM] * 3, out_specs=[VMEM] * 2,
        scratch_shapes=[
            pltpu.VMEM((1, rows), f32), pltpu.VMEM((TOPK, rows), jnp.int32), pltpu.SemaphoreType.DMA((3,))],
        compiler_params=PARAMS, cost_estimate=pl.CostEstimate(flops=4000000000, bytes_accessed=12000000, transcendentals=0), name="stage",
    )(*held[:3])
    far_info = swap(near_info, 1, 1)

    got = swap(references, *rounds[0])
    gathered = join(own, got)
    p_own, own_flipped = pl.pallas_call(
        flip_kernel,
        out_shape=(jax.ShapeDtypeStruct((rows, width), bf16), jax.ShapeDtypeStruct((width, rows), bf16)),
        in_specs=[VMEM, HBM], out_specs=[VMEM] * 2, scratch_shapes=[pltpu.SemaphoreType.DMA((FLIPS,))],
        compiler_params=PARAMS, cost_estimate=pl.CostEstimate(flops=4000000000, bytes_accessed=12000000, transcendentals=0), name="flip",
    )(gathered, held[3])
    for r, pair in enumerate(rounds[1:], 1):
        got = swap(gathered, *pair)
        if r < len(rounds) - 1:
            gathered = join(gathered, got, own_flipped, far_info)

    turned = pltpu.VMEM((ROT * half, width), bf16)
    cost = pl.CostEstimate(
        flops=2 * ROT * half * both * width, bytes_accessed=4 * both * width, transcendentals=0)
    info = (near_info, far_info)
    early, far_flipped = pl.pallas_call(
        early_kernel,
        out_shape=(jax.ShapeDtypeStruct((ROT, half, both), f32), jax.ShapeDtypeStruct((width, rows), bf16)),
        in_specs=[VMEM] * 5, out_specs=[VMEM] * 2, scratch_shapes=[turned],
        compiler_params=PARAMS, cost_estimate=cost, name="early",
    )(gathered, own_flipped, p_far, *info)
    late, near = pl.pallas_call(
        late_kernel,
        out_shape=(jax.ShapeDtypeStruct((ROT, half, both), f32), jax.ShapeDtypeStruct((1, both), f32)),
        in_specs=[VMEM] * 6, out_specs=[VMEM] * 2, scratch_shapes=[turned],
        compiler_params=PARAMS, cost_estimate=cost, name="late",
    )(got, own_flipped, far_flipped, *info, early)
    other = swap(near, 1, 1)
    shared = (p_own, p_far, *info)

    send = pl.pallas_call(
        functools.partial(back_kernel, bits, owned, half),
        out_shape=jax.ShapeDtypeStruct((half, wide), bf16),
        in_specs=[VMEM] * 7, out_specs=VMEM,
        compiler_params=PARAMS, cost_estimate=cost, name="back_send",
    )(late, near, other, *shared)
    keep, log_evidence = pl.pallas_call(
        functools.partial(back_kernel, bits, owned, 0),
        out_shape=(jax.ShapeDtypeStruct((half, wide), f32), jax.ShapeDtypeStruct((1, rows), f32)),
        in_specs=[VMEM] * 7, out_specs=[VMEM] * 2,
        compiler_params=PARAMS, cost_estimate=cost, name="back_keep",
    )(early, near, other, *shared)

    for r, pair in enumerate(rounds[::-1], 1):
        got = swap(send, *pair)
        if r < len(rounds):
            total = keep + got.astype(f32)
            part = total.shape[0] // 2
            keep, send = total[:part], total[part:].astype(bf16)
    sums, mass = pl.pallas_call(
        last_kernel,
        out_shape=(jax.ShapeDtypeStruct((owned, width), f32), jax.ShapeDtypeStruct((owned,), f32)),
        in_specs=[VMEM] * 2,
        out_specs=[VMEM, pl.BlockSpec(memory_space=pltpu.SMEM)],
        compiler_params=PARAMS, name="last",
    )(keep, got)
    return sums, mass, log_evidence[0]


def solution(mesh):
    placed = (
        P(("parts", "blk"), None),
        P(("parts", "blk"), None),
        P(("parts", "blk")),
        P(("parts", "blk"), None),
    )
    return jax.shard_map(
        local,
        mesh=mesh,
        in_specs=placed,
        out_specs=(P(("parts", "blk"), None), P(("parts", "blk")), P(("parts", "blk"))),
        check_vma=False,
    )
```

```python
import functools

import jax
import jax.numpy as jnp
from jax import lax
from jax.experimental import pallas as pl
from jax.experimental.pallas import tpu as pltpu
from jax.sharding import PartitionSpec as P

ROT = 12
CYCLES = 12
ANGLES = 384
TOPK = 2
WIDTH = CYCLES * ANGLES
LANES = 128
STEP = ANGLES // ROT
FINE = LANES // STEP
COARSE = ROT // FINE
VMEM = pl.BlockSpec(memory_space=pltpu.VMEM)
HBM = pl.BlockSpec(memory_space=pltpu.HBM)
PARAMS = pltpu.CompilerParams(vmem_limit_bytes=40 * 1024 * 1024)


def stage_kernel(refs, noise, names, particles, refs_ref, packed_ref, p_ref, noise_ref, names_ref, sems):
    copies = [
        pltpu.make_async_copy(src, dst, sems.at[i])
        for i, (src, dst) in enumerate(
            ((refs, refs_ref), (noise, noise_ref), (names, names_ref), (particles, p_ref)))
    ]
    for copy in copies:
        copy.start()
    for copy in copies[:3]:
        copy.wait()
    packed_ref[0:1, :] = noise_ref[...]
    packed_ref[1:1 + TOPK, :] = names_ref[...].astype(jnp.float32)
    copies[3].wait()


def flip(p_ref, flipped_ref):
    for at in range(0, WIDTH, LANES):
        flipped_ref[at:at + LANES, :] = p_ref[:, at:at + LANES].T


def flip_kernel(after_ref, p_ref, flipped_ref):
    flip(p_ref, flipped_ref)


def join_kernel(held_ref, got_ref, *rest):
    out_ref = rest[-1]
    count = held_ref.shape[0]
    out_ref[0:count, :] = held_ref[...]
    out_ref[count:2 * count, :] = got_ref[...]


def particles_of(own_ref, far_ref, start, size):
    return jnp.concatenate([own_ref[:, start:start + size], far_ref[:, start:start + size]], axis=0)


def score(refs_ref, own_flipped, far_flipped, near_info, far_info, turned_ref):
    classes = refs_ref.shape[0]
    group = FINE * classes
    energy = jnp.zeros((classes, LANES), jnp.float32)
    for c in range(CYCLES):
        cube = refs_ref[:, c * ANGLES:(c + 1) * ANGLES].astype(jnp.float32)
        for v in range(COARSE):
            piece = cube[:, v * LANES:(v + 1) * LANES]
            energy = energy + piece * piece
        moved = [cube] + [pltpu.roll(cube, s * STEP, 1) for s in range(1, FINE)]
        moved = jnp.concatenate(moved, axis=0).astype(jnp.bfloat16)
        for q in range(COARSE):
            for v in range(COARSE):
                at = c * ANGLES + (v + q) % COARSE * LANES
                turned_ref[q * group:(q + 1) * group, at:at + LANES] = moved[:, v * LANES:(v + 1) * LANES]
    energy = jnp.sum(energy, axis=1, keepdims=True)
    dots = lax.dot_general(
        turned_ref[...], jnp.concatenate([own_flipped[...], far_flipped[...]], axis=1),
        (((1,), (0,)), ((), ())), preferred_element_type=jnp.float32,
    )
    dots = dots.reshape(ROT, classes, dots.shape[1])
    noise = jnp.concatenate([near_info[0:1, :], far_info[0:1, :]], axis=1)
    return noise[None] * (dots - 0.5 * energy[None])


def early_kernel(refs_ref, own_flipped, far_ref, near_info, far_info, logits_ref, far_flipped, turned_ref):
    flip(far_ref, far_flipped)
    logits_ref[...] = score(refs_ref, own_flipped, far_flipped, near_info, far_info, turned_ref)


def late_kernel(refs_ref, own_flipped, far_flipped, near_info, far_info, early_ref, logits_ref, part_ref, turned_ref):
    late = score(refs_ref, own_flipped, far_flipped, near_info, far_info, turned_ref)
    logits_ref[...] = late
    early = early_ref[...]
    top = jnp.maximum(jnp.max(late, axis=0), jnp.max(early, axis=0))
    top = jnp.max(top, axis=0, keepdims=True)
    total = jnp.sum(jnp.exp(late - top[None]), axis=0) + jnp.sum(jnp.exp(early - top[None]), axis=0)
    part_ref[...] = top + jnp.log(jnp.sum(total, axis=0, keepdims=True))


def back_kernel(bits, owned, first, logits_ref, near_ref, other_ref, own_ref, far_ref, near_info, far_info,
                sums_ref, log_ref=None):
    classes, rows = logits_ref.shape[1:]
    here = own_ref.shape[0]
    me = lax.axis_index("blk")
    near = near_ref[...]
    far = jnp.concatenate([other_ref[:, here:], other_ref[:, :here]], axis=1)
    top = jnp.maximum(near, far)
    log_evidence = top + jnp.log(jnp.exp(near - top) + jnp.exp(far - top))
    if log_ref is not None:
        log_ref[...] = log_evidence[:, :log_ref.shape[1]]

    row = lax.broadcasted_iota(jnp.int32, (classes, rows), 0) + first
    place = row // owned
    mixed = jnp.zeros_like(place)
    color = me
    for i in range(1, bits):
        color = color ^ (me >> i)
    for i, (even, odd) in enumerate(offsets(bits)):
        mixed = mixed ^ ((place >> i) & 1) * jnp.where(color % 2 == 0, even, odd)
    ident = (mixed ^ me) * owned + row % owned
    names = jnp.concatenate([near_info[...], far_info[...]], axis=1).astype(jnp.int32)
    named = ident == names[1:2, :]
    for j in range(1, TOPK):
        named = named | (ident == names[1 + j:2 + j, :])
    post = jnp.where(named[None], jnp.exp(logits_ref[...] - log_evidence[None]), 0.0)
    weights = jnp.sum(post, axis=0).astype(jnp.bfloat16).astype(jnp.float32)
    mass = jnp.broadcast_to(jnp.sum(weights, axis=1, keepdims=True), (classes, LANES))
    sums_ref[:, WIDTH:] = mass.astype(sums_ref.dtype)

    count = ROT * classes
    post = post.reshape(count, rows)
    high = post.astype(jnp.bfloat16)
    low = (post - high.astype(jnp.float32)).astype(jnp.bfloat16)
    both = jnp.concatenate([high, low], axis=0)
    group = FINE * classes
    for c in range(0, CYCLES, 2):
        chunk = particles_of(own_ref, far_ref, c * ANGLES, 2 * ANGLES)
        part = jnp.dot(both, chunk, preferred_element_type=jnp.float32)
        part = part[:count] + part[count:]
        for d in range(2):
            blocks = []
            for v in range(COARSE):
                block = None
                for q in range(COARSE):
                    at = d * ANGLES + (v + q) % COARSE * LANES
                    piece = part[q * group:(q + 1) * group, at:at + LANES]
                    block = piece if block is None else block + piece
                blocks.append(block)
            turned = jnp.concatenate(blocks, axis=1)
            summed = turned[:classes]
            for s in range(1, FINE):
                summed = summed + pltpu.roll(turned[s * classes:(s + 1) * classes], ANGLES - s * STEP, 1)
            sums_ref[:, (c + d) * ANGLES:(c + d + 1) * ANGLES] = summed.astype(sums_ref.dtype)


def last_kernel(keep_ref, got_ref, sums_ref, mass_ref):
    owned = sums_ref.shape[0]
    total = keep_ref[0:owned, :] + got_ref[...].astype(jnp.float32)
    sums_ref[...] = total[:, :WIDTH]
    for i in range(owned):
        mass_ref[i] = total[i, WIDTH]


def offsets(bits):
    even = [(1 << b) | 1 for b in range(bits - 1, 0, -1)]
    odd = even[:-2] + even[:-3:-1]
    return list(zip(even, odd))


def local(particles, references, inv_noise, assign):
    rows, width = particles.shape
    owned = references.shape[0]
    devices = lax.axis_size("blk")
    bits = devices.bit_length() - 1
    half = owned * devices // 4
    both = 2 * rows
    wide = width + LANES
    f32, bf16 = jnp.float32, jnp.bfloat16

    def swap(x, even, odd):
        return lax.ppermute(x, "blk", [(i, i ^ (odd if i.bit_count() % 2 else even)) for i in range(devices)])

    def join(*operands):
        held = operands[0]
        return pl.pallas_call(
            join_kernel, out_shape=jax.ShapeDtypeStruct((2 * held.shape[0], width), bf16),
            in_specs=[VMEM] * len(operands), out_specs=VMEM, compiler_params=PARAMS, cost_estimate=pl.CostEstimate(flops=4000000000, bytes_accessed=12000000, transcendentals=0), name="join",
        )(*operands)

    rounds = offsets(bits)
    got = swap(references, *rounds[0])
    p_far = swap(particles, 1, 1)
    held = [pltpu.with_memory_space_constraint(x, pltpu.HBM)
            for x in (references, inv_noise[None, :], assign.T, particles)]
    own, near_info, p_own = pl.pallas_call(
        stage_kernel,
        out_shape=(
            jax.ShapeDtypeStruct((owned, width), bf16),
            jax.ShapeDtypeStruct((1 + TOPK, rows), f32),
            jax.ShapeDtypeStruct((rows, width), bf16),
        ),
        in_specs=[HBM] * 4, out_specs=[VMEM] * 3,
        scratch_shapes=[
            pltpu.VMEM((1, rows), f32), pltpu.VMEM((TOPK, rows), jnp.int32), pltpu.SemaphoreType.DMA((4,))],
        compiler_params=PARAMS, cost_estimate=pl.CostEstimate(flops=4000000000, bytes_accessed=12000000, transcendentals=0), name="stage",
    )(*held)
    far_info = swap(near_info, 1, 1)

    before, gathered = own, join(own, got)
    for pair in rounds[1:-1]:
        before, got = gathered, swap(gathered, *pair)
        gathered = join(before, got)
    parts = swap(before, *rounds[-1]), swap(got, *rounds[-1])
    own_flipped = pl.pallas_call(
        flip_kernel, out_shape=jax.ShapeDtypeStruct((width, rows), bf16),
        in_specs=[VMEM] * 2, out_specs=VMEM, compiler_params=PARAMS, cost_estimate=pl.CostEstimate(flops=4000000000, bytes_accessed=12000000, transcendentals=0), name="flip",
    )(gathered, p_own)

    turned = pltpu.VMEM((ROT * half, width), bf16)
    cost = pl.CostEstimate(
        flops=2 * ROT * half * both * width, bytes_accessed=4 * both * width, transcendentals=0)
    info = (near_info, far_info)
    early, far_flipped = pl.pallas_call(
        early_kernel,
        out_shape=(jax.ShapeDtypeStruct((ROT, half, both), f32), jax.ShapeDtypeStruct((width, rows), bf16)),
        in_specs=[VMEM] * 5, out_specs=[VMEM] * 2, scratch_shapes=[turned],
        compiler_params=PARAMS, cost_estimate=cost, name="early",
    )(gathered, own_flipped, p_far, *info)
    got = join(*parts, far_flipped)
    late, near = pl.pallas_call(
        late_kernel,
        out_shape=(jax.ShapeDtypeStruct((ROT, half, both), f32), jax.ShapeDtypeStruct((1, both), f32)),
        in_specs=[VMEM] * 6, out_specs=[VMEM] * 2, scratch_shapes=[turned],
        compiler_params=PARAMS, cost_estimate=cost, name="late",
    )(got, own_flipped, far_flipped, *info, early)
    other = swap(near, 1, 1)
    shared = (p_own, p_far, *info)

    send = pl.pallas_call(
        functools.partial(back_kernel, bits, owned, half),
        out_shape=jax.ShapeDtypeStruct((half, wide), bf16),
        in_specs=[VMEM] * 7, out_specs=VMEM,
        compiler_params=PARAMS, cost_estimate=cost, name="back_send",
    )(late, near, other, *shared)
    keep, log_evidence = pl.pallas_call(
        functools.partial(back_kernel, bits, owned, 0),
        out_shape=(jax.ShapeDtypeStruct((half, wide), f32), jax.ShapeDtypeStruct((1, rows), f32)),
        in_specs=[VMEM] * 7, out_specs=[VMEM] * 2,
        compiler_params=PARAMS, cost_estimate=cost, name="back_keep",
    )(early, near, other, *shared)

    for r, pair in enumerate(rounds[::-1], 1):
        got = swap(send, *pair)
        if r < len(rounds):
            total = keep + got.astype(f32)
            part = total.shape[0] // 2
            keep, send = total[:part], total[part:].astype(bf16)
    sums, mass = pl.pallas_call(
        last_kernel,
        out_shape=(jax.ShapeDtypeStruct((owned, width), f32), jax.ShapeDtypeStruct((owned,), f32)),
        in_specs=[VMEM] * 2,
        out_specs=[VMEM, pl.BlockSpec(memory_space=pltpu.SMEM)],
        compiler_params=PARAMS, name="last",
    )(keep, got)
    return sums, mass, log_evidence[0]


def solution(mesh):
    placed = (
        P(("parts", "blk"), None),
        P(("parts", "blk"), None),
        P(("parts", "blk")),
        P(("parts", "blk"), None),
    )
    return jax.shard_map(
        local,
        mesh=mesh,
        in_specs=placed,
        out_specs=(P(("parts", "blk"), None), P(("parts", "blk")), P(("parts", "blk"))),
        check_vma=False,
    )
```

```python
import functools

import jax
import jax.numpy as jnp
from jax import lax
from jax.experimental import pallas as pl
from jax.experimental.pallas import tpu as pltpu
from jax.sharding import PartitionSpec as P

ROT = 12
CYCLES = 12
ANGLES = 384
TOPK = 2
WIDTH = CYCLES * ANGLES
LANES = 128
STEP = ANGLES // ROT
FINE = LANES // STEP
COARSE = ROT // FINE
VMEM = pl.BlockSpec(memory_space=pltpu.VMEM)
HBM = pl.BlockSpec(memory_space=pltpu.HBM)
PARAMS = pltpu.CompilerParams(vmem_limit_bytes=40 * 1024 * 1024)


def stage_kernel(refs, noise, names, particles, refs_ref, packed_ref, p_ref, noise_ref, names_ref, sems):
    copies = [
        pltpu.make_async_copy(src, dst, sems.at[i])
        for i, (src, dst) in enumerate(
            ((refs, refs_ref), (noise, noise_ref), (names, names_ref), (particles, p_ref)))
    ]
    for copy in copies:
        copy.start()
    for copy in copies[:3]:
        copy.wait()
    packed_ref[0:1, :] = noise_ref[...]
    packed_ref[1:1 + TOPK, :] = names_ref[...].astype(jnp.float32)
    copies[3].wait()


def flip(p_ref, flipped_ref):
    for at in range(0, WIDTH, LANES):
        flipped_ref[at:at + LANES, :] = p_ref[:, at:at + LANES].T


def flip_kernel(after_ref, p_ref, flipped_ref):
    flip(p_ref, flipped_ref)


def join_kernel(held_ref, got_ref, *rest):
    out_ref = rest[-1]
    count = held_ref.shape[0]
    out_ref[0:count, :] = held_ref[...]
    out_ref[count:2 * count, :] = got_ref[...]


def particles_of(own_ref, far_ref, start, size):
    return jnp.concatenate([own_ref[:, start:start + size], far_ref[:, start:start + size]], axis=0)


def score(refs_ref, own_flipped, far_flipped, near_info, far_info, turned_ref):
    classes = refs_ref.shape[0]
    group = FINE * classes
    energy = jnp.zeros((classes, LANES), jnp.float32)
    for c in range(CYCLES):
        cube = refs_ref[:, c * ANGLES:(c + 1) * ANGLES].astype(jnp.float32)
        for v in range(COARSE):
            piece = cube[:, v * LANES:(v + 1) * LANES]
            energy = energy + piece * piece
        moved = [cube] + [pltpu.roll(cube, s * STEP, 1) for s in range(1, FINE)]
        moved = jnp.concatenate(moved, axis=0).astype(jnp.bfloat16)
        for q in range(COARSE):
            for v in range(COARSE):
                at = c * ANGLES + (v + q) % COARSE * LANES
                turned_ref[q * group:(q + 1) * group, at:at + LANES] = moved[:, v * LANES:(v + 1) * LANES]
    energy = jnp.sum(energy, axis=1, keepdims=True)
    dots = lax.dot_general(
        turned_ref[...], jnp.concatenate([own_flipped[...], far_flipped[...]], axis=1),
        (((1,), (0,)), ((), ())), preferred_element_type=jnp.float32,
    )
    dots = dots.reshape(ROT, classes, dots.shape[1])
    noise = jnp.concatenate([near_info[0:1, :], far_info[0:1, :]], axis=1)
    return noise[None] * (dots - 0.5 * energy[None])


def sums_of(logits):
    top = jnp.max(jnp.max(logits, axis=0), axis=0, keepdims=True)
    total = jnp.sum(jnp.sum(jnp.exp(logits - top[None]), axis=0), axis=0, keepdims=True)
    return top, total


def early_kernel(refs_ref, own_flipped, far_ref, near_info, far_info, logits_ref, far_flipped, part_ref, turned_ref):
    flip(far_ref, far_flipped)
    early = score(refs_ref, own_flipped, far_flipped, near_info, far_info, turned_ref)
    logits_ref[...] = early
    top, total = sums_of(early)
    part_ref[...] = jnp.concatenate([top, total], axis=0)


def late_kernel(refs_ref, own_flipped, far_flipped, near_info, far_info, early_ref, logits_ref, part_ref, turned_ref):
    late = score(refs_ref, own_flipped, far_flipped, near_info, far_info, turned_ref)
    logits_ref[...] = late
    top, total = sums_of(late)
    top_early, total_early = early_ref[0:1, :], early_ref[1:2, :]
    both = jnp.maximum(top, top_early)
    total = total * jnp.exp(top - both) + total_early * jnp.exp(top_early - both)
    part_ref[...] = both + jnp.log(total)


def back_kernel(bits, owned, first, logits_ref, near_ref, other_ref, own_ref, far_ref, near_info, far_info,
                sums_ref, log_ref=None):
    classes, rows = logits_ref.shape[1:]
    here = own_ref.shape[0]
    me = lax.axis_index("blk")
    near = near_ref[...]
    far = jnp.concatenate([other_ref[:, here:], other_ref[:, :here]], axis=1)
    top = jnp.maximum(near, far)
    log_evidence = top + jnp.log(jnp.exp(near - top) + jnp.exp(far - top))
    if log_ref is not None:
        log_ref[...] = log_evidence[:, :log_ref.shape[1]]

    row = lax.broadcasted_iota(jnp.int32, (classes, rows), 0) + first
    place = row // owned
    mixed = jnp.zeros_like(place)
    color = me
    for i in range(1, bits):
        color = color ^ (me >> i)
    for i, (even, odd) in enumerate(offsets(bits)):
        mixed = mixed ^ ((place >> i) & 1) * jnp.where(color % 2 == 0, even, odd)
    ident = (mixed ^ me) * owned + row % owned
    names = jnp.concatenate([near_info[...], far_info[...]], axis=1).astype(jnp.int32)
    named = ident == names[1:2, :]
    for j in range(1, TOPK):
        named = named | (ident == names[1 + j:2 + j, :])
    post = jnp.where(named[None], jnp.exp(logits_ref[...] - log_evidence[None]), 0.0)
    weights = jnp.sum(post, axis=0).astype(jnp.bfloat16).astype(jnp.float32)
    mass = jnp.broadcast_to(jnp.sum(weights, axis=1, keepdims=True), (classes, LANES))
    sums_ref[:, WIDTH:] = mass.astype(sums_ref.dtype)

    count = ROT * classes
    post = post.reshape(count, rows)
    high = post.astype(jnp.bfloat16)
    low = (post - high.astype(jnp.float32)).astype(jnp.bfloat16)
    both = jnp.concatenate([high, low], axis=0)
    group = FINE * classes
    for c in range(0, CYCLES, 2):
        chunk = particles_of(own_ref, far_ref, c * ANGLES, 2 * ANGLES)
        part = jnp.dot(both, chunk, preferred_element_type=jnp.float32)
        part = part[:count] + part[count:]
        for d in range(2):
            blocks = []
            for v in range(COARSE):
                block = None
                for q in range(COARSE):
                    at = d * ANGLES + (v + q) % COARSE * LANES
                    piece = part[q * group:(q + 1) * group, at:at + LANES]
                    block = piece if block is None else block + piece
                blocks.append(block)
            turned = jnp.concatenate(blocks, axis=1)
            summed = turned[:classes]
            for s in range(1, FINE):
                summed = summed + pltpu.roll(turned[s * classes:(s + 1) * classes], ANGLES - s * STEP, 1)
            sums_ref[:, (c + d) * ANGLES:(c + d + 1) * ANGLES] = summed.astype(sums_ref.dtype)


def last_kernel(keep_ref, got_ref, sums_ref, mass_ref):
    owned = sums_ref.shape[0]
    total = keep_ref[0:owned, :] + got_ref[...].astype(jnp.float32)
    sums_ref[...] = total[:, :WIDTH]
    for i in range(owned):
        mass_ref[i] = total[i, WIDTH]


def offsets(bits):
    even = [(1 << b) | 1 for b in range(bits - 1, 0, -1)]
    odd = even[:-2] + even[:-3:-1]
    return list(zip(even, odd))


def local(particles, references, inv_noise, assign):
    rows, width = particles.shape
    owned = references.shape[0]
    devices = lax.axis_size("blk")
    bits = devices.bit_length() - 1
    half = owned * devices // 4
    both = 2 * rows
    wide = width + LANES
    f32, bf16 = jnp.float32, jnp.bfloat16

    def swap(x, even, odd):
        return lax.ppermute(x, "blk", [(i, i ^ (odd if i.bit_count() % 2 else even)) for i in range(devices)])

    def join(*operands):
        held = operands[0]
        return pl.pallas_call(
            join_kernel, out_shape=jax.ShapeDtypeStruct((2 * held.shape[0], width), bf16),
            in_specs=[VMEM] * len(operands), out_specs=VMEM, compiler_params=PARAMS, cost_estimate=pl.CostEstimate(flops=4000000000, bytes_accessed=12000000, transcendentals=0), name="join",
        )(*operands)

    rounds = offsets(bits)
    got = swap(references, *rounds[0])
    p_far = swap(particles, 1, 1)
    held = [pltpu.with_memory_space_constraint(x, pltpu.HBM)
            for x in (references, inv_noise[None, :], assign.T, particles)]
    own, near_info, p_own = pl.pallas_call(
        stage_kernel,
        out_shape=(
            jax.ShapeDtypeStruct((owned, width), bf16),
            jax.ShapeDtypeStruct((1 + TOPK, rows), f32),
            jax.ShapeDtypeStruct((rows, width), bf16),
        ),
        in_specs=[HBM] * 4, out_specs=[VMEM] * 3,
        scratch_shapes=[
            pltpu.VMEM((1, rows), f32), pltpu.VMEM((TOPK, rows), jnp.int32), pltpu.SemaphoreType.DMA((4,))],
        compiler_params=PARAMS, cost_estimate=pl.CostEstimate(flops=4000000000, bytes_accessed=12000000, transcendentals=0), name="stage",
    )(*held)
    far_info = swap(near_info, 1, 1)

    before, gathered = own, join(own, got)
    for pair in rounds[1:-1]:
        before, got = gathered, swap(gathered, *pair)
        gathered = join(before, got)
    parts = swap(before, *rounds[-1]), swap(got, *rounds[-1])
    own_flipped = pl.pallas_call(
        flip_kernel, out_shape=jax.ShapeDtypeStruct((width, rows), bf16),
        in_specs=[VMEM] * 2, out_specs=VMEM, compiler_params=PARAMS, cost_estimate=pl.CostEstimate(flops=4000000000, bytes_accessed=12000000, transcendentals=0), name="flip",
    )(gathered, p_own)

    turned = pltpu.VMEM((ROT * half, width), bf16)
    cost = pl.CostEstimate(
        flops=2 * ROT * half * both * width, bytes_accessed=4 * both * width, transcendentals=0)
    info = (near_info, far_info)
    early, far_flipped, early_part = pl.pallas_call(
        early_kernel,
        out_shape=(
            jax.ShapeDtypeStruct((ROT, half, both), f32),
            jax.ShapeDtypeStruct((width, rows), bf16),
            jax.ShapeDtypeStruct((2, both), f32),
        ),
        in_specs=[VMEM] * 5, out_specs=[VMEM] * 3, scratch_shapes=[turned],
        compiler_params=PARAMS, cost_estimate=cost, name="early",
    )(gathered, own_flipped, p_far, *info)
    got = join(*parts, far_flipped)
    late, near = pl.pallas_call(
        late_kernel,
        out_shape=(jax.ShapeDtypeStruct((ROT, half, both), f32), jax.ShapeDtypeStruct((1, both), f32)),
        in_specs=[VMEM] * 6, out_specs=[VMEM] * 2, scratch_shapes=[turned],
        compiler_params=PARAMS, cost_estimate=cost, name="late",
    )(got, own_flipped, far_flipped, *info, early_part)
    other = swap(near, 1, 1)
    shared = (p_own, p_far, *info)

    send = pl.pallas_call(
        functools.partial(back_kernel, bits, owned, half),
        out_shape=jax.ShapeDtypeStruct((half, wide), bf16),
        in_specs=[VMEM] * 7, out_specs=VMEM,
        compiler_params=PARAMS, cost_estimate=cost, name="back_send",
    )(late, near, other, *shared)
    keep, log_evidence = pl.pallas_call(
        functools.partial(back_kernel, bits, owned, 0),
        out_shape=(jax.ShapeDtypeStruct((half, wide), f32), jax.ShapeDtypeStruct((1, rows), f32)),
        in_specs=[VMEM] * 7, out_specs=[VMEM] * 2,
        compiler_params=PARAMS, cost_estimate=cost, name="back_keep",
    )(early, near, other, *shared)

    for r, pair in enumerate(rounds[::-1], 1):
        got = swap(send, *pair)
        if r < len(rounds):
            total = keep + got.astype(f32)
            part = total.shape[0] // 2
            keep, send = total[:part], total[part:].astype(bf16)
    sums, mass = pl.pallas_call(
        last_kernel,
        out_shape=(jax.ShapeDtypeStruct((owned, width), f32), jax.ShapeDtypeStruct((owned,), f32)),
        in_specs=[VMEM] * 2,
        out_specs=[VMEM, pl.BlockSpec(memory_space=pltpu.SMEM)],
        compiler_params=PARAMS, name="last",
    )(keep, got)
    return sums, mass, log_evidence[0]


def solution(mesh):
    placed = (
        P(("parts", "blk"), None),
        P(("parts", "blk"), None),
        P(("parts", "blk")),
        P(("parts", "blk"), None),
    )
    return jax.shard_map(
        local,
        mesh=mesh,
        in_specs=placed,
        out_specs=(P(("parts", "blk"), None), P(("parts", "blk")), P(("parts", "blk"))),
        check_vma=False,
    )
```

```python
import functools

import jax
import jax.numpy as jnp
from jax import lax
from jax.experimental import pallas as pl
from jax.experimental.pallas import tpu as pltpu
from jax.sharding import PartitionSpec as P

ROT = 12
CYCLES = 12
ANGLES = 384
TOPK = 2
WIDTH = CYCLES * ANGLES
LANES = 128
STEP = ANGLES // ROT
FINE = LANES // STEP
COARSE = ROT // FINE
VMEM = pl.BlockSpec(memory_space=pltpu.VMEM)
HBM = pl.BlockSpec(memory_space=pltpu.HBM)
PARAMS = pltpu.CompilerParams(vmem_limit_bytes=40 * 1024 * 1024)


def stage_kernel(refs, noise, names, particles, refs_ref, packed_ref, p_ref, noise_ref, names_ref, sems):
    copies = [
        pltpu.make_async_copy(src, dst, sems.at[i])
        for i, (src, dst) in enumerate(
            ((refs, refs_ref), (noise, noise_ref), (names, names_ref), (particles, p_ref)))
    ]
    for copy in copies:
        copy.start()
    for copy in copies[:3]:
        copy.wait()
    packed_ref[0:1, :] = noise_ref[...]
    packed_ref[1:1 + TOPK, :] = names_ref[...].astype(jnp.float32)
    copies[3].wait()


def flip(p_ref, flipped_ref):
    for at in range(0, WIDTH, LANES):
        flipped_ref[at:at + LANES, :] = p_ref[:, at:at + LANES].T


def flip_kernel(after_ref, p_ref, flipped_ref):
    flip(p_ref, flipped_ref)


def join_kernel(held_ref, got_ref, *rest):
    out_ref = rest[-1]
    count = held_ref.shape[0]
    out_ref[0:count, :] = held_ref[...]
    out_ref[count:2 * count, :] = got_ref[...]


def particles_of(own_ref, far_ref, start, size):
    return jnp.concatenate([own_ref[:, start:start + size], far_ref[:, start:start + size]], axis=0)


def score(refs_ref, own_flipped, far_flipped, near_info, far_info, turned_ref):
    classes = refs_ref.shape[0]
    group = FINE * classes
    energy = jnp.zeros((classes, LANES), jnp.float32)
    for c in range(CYCLES):
        cube = refs_ref[:, c * ANGLES:(c + 1) * ANGLES].astype(jnp.float32)
        for v in range(COARSE):
            piece = cube[:, v * LANES:(v + 1) * LANES]
            energy = energy + piece * piece
        moved = [cube] + [pltpu.roll(cube, s * STEP, 1) for s in range(1, FINE)]
        moved = jnp.concatenate(moved, axis=0).astype(jnp.bfloat16)
        for q in range(COARSE):
            for v in range(COARSE):
                at = c * ANGLES + (v + q) % COARSE * LANES
                turned_ref[q * group:(q + 1) * group, at:at + LANES] = moved[:, v * LANES:(v + 1) * LANES]
    energy = jnp.sum(energy, axis=1, keepdims=True)
    dots = lax.dot_general(
        turned_ref[...], jnp.concatenate([own_flipped[...], far_flipped[...]], axis=1),
        (((1,), (0,)), ((), ())), preferred_element_type=jnp.float32,
    )
    dots = dots.reshape(ROT, classes, dots.shape[1])
    noise = jnp.concatenate([near_info[0:1, :], far_info[0:1, :]], axis=1)
    return noise[None] * (dots - 0.5 * energy[None])


def early_kernel(refs_ref, own_flipped, far_ref, near_info, far_info, logits_ref, far_flipped, turned_ref):
    flip(far_ref, far_flipped)
    logits_ref[...] = score(refs_ref, own_flipped, far_flipped, near_info, far_info, turned_ref)


def late_kernel(refs_ref, own_flipped, far_flipped, near_info, far_info, early_ref, logits_ref, part_ref, turned_ref):
    late = score(refs_ref, own_flipped, far_flipped, near_info, far_info, turned_ref)
    logits_ref[...] = late
    early = early_ref[...]
    top = jnp.maximum(jnp.max(late, axis=0), jnp.max(early, axis=0))
    top = jnp.max(top, axis=0, keepdims=True)
    total = jnp.sum(jnp.exp(late - top[None]), axis=0) + jnp.sum(jnp.exp(early - top[None]), axis=0)
    part_ref[...] = top + jnp.log(jnp.sum(total, axis=0, keepdims=True))


def back_kernel(bits, owned, first, logits_ref, near_ref, other_ref, own_ref, far_ref, near_info, far_info,
                sums_ref, log_ref=None):
    classes, rows = logits_ref.shape[1:]
    here = own_ref.shape[0]
    me = lax.axis_index("blk")
    near = near_ref[...]
    far = jnp.concatenate([other_ref[:, here:], other_ref[:, :here]], axis=1)
    top = jnp.maximum(near, far)
    log_evidence = top + jnp.log(jnp.exp(near - top) + jnp.exp(far - top))
    if log_ref is not None:
        log_ref[...] = log_evidence[:, :log_ref.shape[1]]

    row = lax.broadcasted_iota(jnp.int32, (classes, rows), 0) + first
    place = row // owned
    mixed = jnp.zeros_like(place)
    color = me
    for i in range(1, bits):
        color = color ^ (me >> i)
    for i, (even, odd) in enumerate(offsets(bits)):
        mixed = mixed ^ ((place >> i) & 1) * jnp.where(color % 2 == 0, even, odd)
    ident = (mixed ^ me) * owned + row % owned
    names = jnp.concatenate([near_info[...], far_info[...]], axis=1).astype(jnp.int32)
    named = ident == names[1:2, :]
    for j in range(1, TOPK):
        named = named | (ident == names[1 + j:2 + j, :])
    post = jnp.where(named[None], jnp.exp(logits_ref[...] - log_evidence[None]), 0.0)
    weights = jnp.sum(post, axis=0).astype(jnp.bfloat16).astype(jnp.float32)
    mass = jnp.broadcast_to(jnp.sum(weights, axis=1, keepdims=True), (classes, LANES))
    sums_ref[:, WIDTH:] = mass.astype(sums_ref.dtype)

    count = ROT * classes
    post = post.reshape(count, rows)
    high = post.astype(jnp.bfloat16)
    low = (post - high.astype(jnp.float32)).astype(jnp.bfloat16)
    both = jnp.concatenate([high, low], axis=0)
    group = FINE * classes
    parts = []
    for c in range(0, CYCLES, 2):
        chunk = particles_of(own_ref, far_ref, c * ANGLES, 2 * ANGLES)
        parts.append(jnp.dot(both, chunk, preferred_element_type=jnp.float32))
    for c in range(0, CYCLES, 2):
        part = parts[c // 2]
        part = part[:count] + part[count:]
        for d in range(2):
            blocks = []
            for v in range(COARSE):
                block = None
                for q in range(COARSE):
                    at = d * ANGLES + (v + q) % COARSE * LANES
                    piece = part[q * group:(q + 1) * group, at:at + LANES]
                    block = piece if block is None else block + piece
                blocks.append(block)
            turned = jnp.concatenate(blocks, axis=1)
            summed = turned[:classes]
            for s in range(1, FINE):
                summed = summed + pltpu.roll(turned[s * classes:(s + 1) * classes], ANGLES - s * STEP, 1)
            sums_ref[:, (c + d) * ANGLES:(c + d + 1) * ANGLES] = summed.astype(sums_ref.dtype)


def last_kernel(keep_ref, got_ref, sums_ref, mass_ref):
    owned = sums_ref.shape[0]
    total = keep_ref[0:owned, :] + got_ref[...].astype(jnp.float32)
    sums_ref[...] = total[:, :WIDTH]
    for i in range(owned):
        mass_ref[i] = total[i, WIDTH]


def offsets(bits):
    even = [(1 << b) | 1 for b in range(bits - 1, 0, -1)]
    odd = even[:-2] + even[:-3:-1]
    return list(zip(even, odd))


def local(particles, references, inv_noise, assign):
    rows, width = particles.shape
    owned = references.shape[0]
    devices = lax.axis_size("blk")
    bits = devices.bit_length() - 1
    half = owned * devices // 4
    both = 2 * rows
    wide = width + LANES
    f32, bf16 = jnp.float32, jnp.bfloat16

    def swap(x, even, odd):
        return lax.ppermute(x, "blk", [(i, i ^ (odd if i.bit_count() % 2 else even)) for i in range(devices)])

    def join(*operands):
        held = operands[0]
        return pl.pallas_call(
            join_kernel, out_shape=jax.ShapeDtypeStruct((2 * held.shape[0], width), bf16),
            in_specs=[VMEM] * len(operands), out_specs=VMEM, compiler_params=PARAMS, cost_estimate=pl.CostEstimate(flops=4000000000, bytes_accessed=12000000, transcendentals=0), name="join",
        )(*operands)

    rounds = offsets(bits)
    got = swap(references, *rounds[0])
    p_far = swap(particles, 1, 1)
    held = [pltpu.with_memory_space_constraint(x, pltpu.HBM)
            for x in (references, inv_noise[None, :], assign.T, particles)]
    own, near_info, p_own = pl.pallas_call(
        stage_kernel,
        out_shape=(
            jax.ShapeDtypeStruct((owned, width), bf16),
            jax.ShapeDtypeStruct((1 + TOPK, rows), f32),
            jax.ShapeDtypeStruct((rows, width), bf16),
        ),
        in_specs=[HBM] * 4, out_specs=[VMEM] * 3,
        scratch_shapes=[
            pltpu.VMEM((1, rows), f32), pltpu.VMEM((TOPK, rows), jnp.int32), pltpu.SemaphoreType.DMA((4,))],
        compiler_params=PARAMS, cost_estimate=pl.CostEstimate(flops=4000000000, bytes_accessed=12000000, transcendentals=0), name="stage",
    )(*held)
    far_info = swap(near_info, 1, 1)

    before, gathered = own, join(own, got)
    for pair in rounds[1:-1]:
        before, got = gathered, swap(gathered, *pair)
        gathered = join(before, got)
    parts = swap(before, *rounds[-1]), swap(got, *rounds[-1])
    own_flipped = pl.pallas_call(
        flip_kernel, out_shape=jax.ShapeDtypeStruct((width, rows), bf16),
        in_specs=[VMEM] * 2, out_specs=VMEM, compiler_params=PARAMS, cost_estimate=pl.CostEstimate(flops=4000000000, bytes_accessed=12000000, transcendentals=0), name="flip",
    )(gathered, p_own)

    turned = pltpu.VMEM((ROT * half, width), bf16)
    cost = pl.CostEstimate(
        flops=2 * ROT * half * both * width, bytes_accessed=4 * both * width, transcendentals=0)
    info = (near_info, far_info)
    early, far_flipped = pl.pallas_call(
        early_kernel,
        out_shape=(jax.ShapeDtypeStruct((ROT, half, both), f32), jax.ShapeDtypeStruct((width, rows), bf16)),
        in_specs=[VMEM] * 5, out_specs=[VMEM] * 2, scratch_shapes=[turned],
        compiler_params=PARAMS, cost_estimate=cost, name="early",
    )(gathered, own_flipped, p_far, *info)
    got = join(*parts, far_flipped)
    late, near = pl.pallas_call(
        late_kernel,
        out_shape=(jax.ShapeDtypeStruct((ROT, half, both), f32), jax.ShapeDtypeStruct((1, both), f32)),
        in_specs=[VMEM] * 6, out_specs=[VMEM] * 2, scratch_shapes=[turned],
        compiler_params=PARAMS, cost_estimate=cost, name="late",
    )(got, own_flipped, far_flipped, *info, early)
    other = swap(near, 1, 1)
    shared = (p_own, p_far, *info)

    send = pl.pallas_call(
        functools.partial(back_kernel, bits, owned, half),
        out_shape=jax.ShapeDtypeStruct((half, wide), bf16),
        in_specs=[VMEM] * 7, out_specs=VMEM,
        compiler_params=PARAMS, cost_estimate=cost, name="back_send",
    )(late, near, other, *shared)
    keep, log_evidence = pl.pallas_call(
        functools.partial(back_kernel, bits, owned, 0),
        out_shape=(jax.ShapeDtypeStruct((half, wide), f32), jax.ShapeDtypeStruct((1, rows), f32)),
        in_specs=[VMEM] * 7, out_specs=[VMEM] * 2,
        compiler_params=PARAMS, cost_estimate=cost, name="back_keep",
    )(early, near, other, *shared)

    for r, pair in enumerate(rounds[::-1], 1):
        got = swap(send, *pair)
        if r < len(rounds):
            total = keep + got.astype(f32)
            part = total.shape[0] // 2
            keep, send = total[:part], total[part:].astype(bf16)
    sums, mass = pl.pallas_call(
        last_kernel,
        out_shape=(jax.ShapeDtypeStruct((owned, width), f32), jax.ShapeDtypeStruct((owned,), f32)),
        in_specs=[VMEM] * 2,
        out_specs=[VMEM, pl.BlockSpec(memory_space=pltpu.SMEM)],
        compiler_params=PARAMS, name="last",
    )(keep, got)
    return sums, mass, log_evidence[0]


def solution(mesh):
    placed = (
        P(("parts", "blk"), None),
        P(("parts", "blk"), None),
        P(("parts", "blk")),
        P(("parts", "blk"), None),
    )
    return jax.shard_map(
        local,
        mesh=mesh,
        in_specs=placed,
        out_specs=(P(("parts", "blk"), None), P(("parts", "blk")), P(("parts", "blk"))),
        check_vma=False,
    )
```

```python
import functools

import jax
import jax.numpy as jnp
from jax import lax
from jax.experimental import pallas as pl
from jax.experimental.pallas import tpu as pltpu
from jax.sharding import PartitionSpec as P

ROT = 12
CYCLES = 12
ANGLES = 384
TOPK = 2
WIDTH = CYCLES * ANGLES
LANES = 128
STEP = ANGLES // ROT
FINE = LANES // STEP
COARSE = ROT // FINE
VMEM = pl.BlockSpec(memory_space=pltpu.VMEM)
HBM = pl.BlockSpec(memory_space=pltpu.HBM)
PARAMS = pltpu.CompilerParams(vmem_limit_bytes=40 * 1024 * 1024)


def stage_kernel(refs, noise, names, particles, refs_ref, packed_ref, p_ref, noise_ref, names_ref, sems):
    copies = [
        pltpu.make_async_copy(src, dst, sems.at[i])
        for i, (src, dst) in enumerate(
            ((refs, refs_ref), (noise, noise_ref), (names, names_ref), (particles, p_ref)))
    ]
    for copy in copies:
        copy.start()
    for copy in copies[:3]:
        copy.wait()
    packed_ref[0:1, :] = noise_ref[...]
    packed_ref[1:1 + TOPK, :] = names_ref[...].astype(jnp.float32)
    copies[3].wait()


def flip(p_ref, flipped_ref):
    for at in range(0, WIDTH, LANES):
        flipped_ref[at:at + LANES, :] = p_ref[:, at:at + LANES].T


def flip_kernel(after_ref, p_ref, flipped_ref):
    flip(p_ref, flipped_ref)


def join_kernel(held_ref, got_ref, *rest):
    out_ref = rest[-1]
    count = held_ref.shape[0]
    out_ref[0:count, :] = held_ref[...]
    out_ref[count:2 * count, :] = got_ref[...]


def particles_of(own_ref, far_ref, start, size):
    return jnp.concatenate([own_ref[:, start:start + size], far_ref[:, start:start + size]], axis=0)


def score(refs_ref, own_flipped, far_flipped, near_info, far_info, turned_ref):
    classes = refs_ref.shape[0]
    group = FINE * classes
    energy = jnp.zeros((classes, LANES), jnp.float32)
    for c in range(CYCLES):
        cube = refs_ref[:, c * ANGLES:(c + 1) * ANGLES].astype(jnp.float32)
        for v in range(COARSE):
            piece = cube[:, v * LANES:(v + 1) * LANES]
            energy = energy + piece * piece
        moved = [cube] + [pltpu.roll(cube, s * STEP, 1) for s in range(1, FINE)]
        moved = jnp.concatenate(moved, axis=0).astype(jnp.bfloat16)
        for q in range(COARSE):
            for v in range(COARSE):
                at = c * ANGLES + (v + q) % COARSE * LANES
                turned_ref[q * group:(q + 1) * group, at:at + LANES] = moved[:, v * LANES:(v + 1) * LANES]
    energy = jnp.sum(energy, axis=1, keepdims=True)
    dots = lax.dot_general(
        turned_ref[...], jnp.concatenate([own_flipped[...], far_flipped[...]], axis=1),
        (((1,), (0,)), ((), ())), preferred_element_type=jnp.float32,
    )
    dots = dots.reshape(ROT, classes, dots.shape[1])
    noise = jnp.concatenate([near_info[0:1, :], far_info[0:1, :]], axis=1)
    return noise[None] * (dots - 0.5 * energy[None])


def sums_of(logits):
    top = jnp.max(jnp.max(logits, axis=0), axis=0, keepdims=True)
    total = jnp.sum(jnp.sum(jnp.exp(logits - top[None]), axis=0), axis=0, keepdims=True)
    return top, total


def early_kernel(refs_ref, own_flipped, far_ref, near_info, far_info, logits_ref, far_flipped, part_ref, turned_ref):
    flip(far_ref, far_flipped)
    early = score(refs_ref, own_flipped, far_flipped, near_info, far_info, turned_ref)
    logits_ref[...] = early
    top, total = sums_of(early)
    part_ref[...] = jnp.concatenate([top, total], axis=0)


def late_kernel(refs_ref, own_flipped, far_flipped, near_info, far_info, early_ref, logits_ref, part_ref, turned_ref):
    late = score(refs_ref, own_flipped, far_flipped, near_info, far_info, turned_ref)
    logits_ref[...] = late
    top, total = sums_of(late)
    top_early, total_early = early_ref[0:1, :], early_ref[1:2, :]
    both = jnp.maximum(top, top_early)
    total = total * jnp.exp(top - both) + total_early * jnp.exp(top_early - both)
    part_ref[...] = both + jnp.log(total)


def back_kernel(bits, owned, first, logits_ref, near_ref, other_ref, own_ref, far_ref, near_info, far_info,
                sums_ref, log_ref=None):
    classes, rows = logits_ref.shape[1:]
    here = own_ref.shape[0]
    me = lax.axis_index("blk")
    near = near_ref[...]
    far = jnp.concatenate([other_ref[:, here:], other_ref[:, :here]], axis=1)
    top = jnp.maximum(near, far)
    log_evidence = top + jnp.log(jnp.exp(near - top) + jnp.exp(far - top))
    if log_ref is not None:
        log_ref[...] = log_evidence[:, :log_ref.shape[1]]

    row = lax.broadcasted_iota(jnp.int32, (classes, rows), 0) + first
    place = row // owned
    mixed = jnp.zeros_like(place)
    color = me
    for i in range(1, bits):
        color = color ^ (me >> i)
    for i, (even, odd) in enumerate(offsets(bits)):
        mixed = mixed ^ ((place >> i) & 1) * jnp.where(color % 2 == 0, even, odd)
    ident = (mixed ^ me) * owned + row % owned
    names = jnp.concatenate([near_info[...], far_info[...]], axis=1).astype(jnp.int32)
    named = ident == names[1:2, :]
    for j in range(1, TOPK):
        named = named | (ident == names[1 + j:2 + j, :])
    post = jnp.where(named[None], jnp.exp(logits_ref[...] - log_evidence[None]), 0.0)
    weights = jnp.sum(post, axis=0).astype(jnp.bfloat16).astype(jnp.float32)
    mass = jnp.broadcast_to(jnp.sum(weights, axis=1, keepdims=True), (classes, LANES))
    sums_ref[:, WIDTH:] = mass.astype(sums_ref.dtype)

    count = ROT * classes
    post = post.reshape(count, rows)
    high = post.astype(jnp.bfloat16)
    low = (post - high.astype(jnp.float32)).astype(jnp.bfloat16)
    both = jnp.concatenate([high, low], axis=0)
    group = FINE * classes
    parts = []
    for c in range(0, CYCLES, 2):
        chunk = particles_of(own_ref, far_ref, c * ANGLES, 2 * ANGLES)
        parts.append(jnp.dot(both, chunk, preferred_element_type=jnp.float32))
    for c in range(0, CYCLES, 2):
        part = parts[c // 2]
        part = part[:count] + part[count:]
        for d in range(2):
            blocks = []
            for v in range(COARSE):
                block = None
                for q in range(COARSE):
                    at = d * ANGLES + (v + q) % COARSE * LANES
                    piece = part[q * group:(q + 1) * group, at:at + LANES]
                    block = piece if block is None else block + piece
                blocks.append(block)
            turned = jnp.concatenate(blocks, axis=1)
            summed = turned[:classes]
            for s in range(1, FINE):
                summed = summed + pltpu.roll(turned[s * classes:(s + 1) * classes], ANGLES - s * STEP, 1)
            sums_ref[:, (c + d) * ANGLES:(c + d + 1) * ANGLES] = summed.astype(sums_ref.dtype)


def last_kernel(keep_ref, got_ref, sums_ref, mass_ref):
    owned = sums_ref.shape[0]
    total = keep_ref[0:owned, :] + got_ref[...].astype(jnp.float32)
    sums_ref[...] = total[:, :WIDTH]
    for i in range(owned):
        mass_ref[i] = total[i, WIDTH]


def offsets(bits):
    even = [(1 << b) | 1 for b in range(bits - 1, 0, -1)]
    odd = even[:-2] + even[:-3:-1]
    return list(zip(even, odd))


def local(particles, references, inv_noise, assign):
    rows, width = particles.shape
    owned = references.shape[0]
    devices = lax.axis_size("blk")
    bits = devices.bit_length() - 1
    half = owned * devices // 4
    both = 2 * rows
    wide = width + LANES
    f32, bf16 = jnp.float32, jnp.bfloat16

    def swap(x, even, odd):
        return lax.ppermute(x, "blk", [(i, i ^ (odd if i.bit_count() % 2 else even)) for i in range(devices)])

    def join(*operands):
        held = operands[0]
        return pl.pallas_call(
            join_kernel, out_shape=jax.ShapeDtypeStruct((2 * held.shape[0], width), bf16),
            in_specs=[VMEM] * len(operands), out_specs=VMEM, compiler_params=PARAMS, cost_estimate=pl.CostEstimate(flops=4000000000, bytes_accessed=12000000, transcendentals=0), name="join",
        )(*operands)

    rounds = offsets(bits)
    got = swap(references, *rounds[0])
    p_far = swap(particles, 1, 1)
    held = [pltpu.with_memory_space_constraint(x, pltpu.HBM)
            for x in (references, inv_noise[None, :], assign.T, particles)]
    own, near_info, p_own = pl.pallas_call(
        stage_kernel,
        out_shape=(
            jax.ShapeDtypeStruct((owned, width), bf16),
            jax.ShapeDtypeStruct((1 + TOPK, rows), f32),
            jax.ShapeDtypeStruct((rows, width), bf16),
        ),
        in_specs=[HBM] * 4, out_specs=[VMEM] * 3,
        scratch_shapes=[
            pltpu.VMEM((1, rows), f32), pltpu.VMEM((TOPK, rows), jnp.int32), pltpu.SemaphoreType.DMA((4,))],
        compiler_params=PARAMS, cost_estimate=pl.CostEstimate(flops=4000000000, bytes_accessed=12000000, transcendentals=0), name="stage",
    )(*held)
    far_info = swap(near_info, 1, 1)

    before, gathered = own, join(own, got)
    for pair in rounds[1:-1]:
        before, got = gathered, swap(gathered, *pair)
        gathered = join(before, got)
    parts = swap(before, *rounds[-1]), swap(got, *rounds[-1])
    own_flipped = pl.pallas_call(
        flip_kernel, out_shape=jax.ShapeDtypeStruct((width, rows), bf16),
        in_specs=[VMEM] * 2, out_specs=VMEM, compiler_params=PARAMS, cost_estimate=pl.CostEstimate(flops=4000000000, bytes_accessed=12000000, transcendentals=0), name="flip",
    )(gathered, p_own)

    turned = pltpu.VMEM((ROT * half, width), bf16)
    cost = pl.CostEstimate(
        flops=2 * ROT * half * both * width, bytes_accessed=4 * both * width, transcendentals=0)
    info = (near_info, far_info)
    early, far_flipped, early_part = pl.pallas_call(
        early_kernel,
        out_shape=(
            jax.ShapeDtypeStruct((ROT, half, both), f32),
            jax.ShapeDtypeStruct((width, rows), bf16),
            jax.ShapeDtypeStruct((2, both), f32),
        ),
        in_specs=[VMEM] * 5, out_specs=[VMEM] * 3, scratch_shapes=[turned],
        compiler_params=PARAMS, cost_estimate=cost, name="early",
    )(gathered, own_flipped, p_far, *info)
    got = join(*parts, far_flipped)
    late, near = pl.pallas_call(
        late_kernel,
        out_shape=(jax.ShapeDtypeStruct((ROT, half, both), f32), jax.ShapeDtypeStruct((1, both), f32)),
        in_specs=[VMEM] * 6, out_specs=[VMEM] * 2, scratch_shapes=[turned],
        compiler_params=PARAMS, cost_estimate=cost, name="late",
    )(got, own_flipped, far_flipped, *info, early_part)
    other = swap(near, 1, 1)
    shared = (p_own, p_far, *info)

    send = pl.pallas_call(
        functools.partial(back_kernel, bits, owned, half),
        out_shape=jax.ShapeDtypeStruct((half, wide), bf16),
        in_specs=[VMEM] * 7, out_specs=VMEM,
        compiler_params=PARAMS, cost_estimate=cost, name="back_send",
    )(late, near, other, *shared)
    keep, log_evidence = pl.pallas_call(
        functools.partial(back_kernel, bits, owned, 0),
        out_shape=(jax.ShapeDtypeStruct((half, wide), f32), jax.ShapeDtypeStruct((1, rows), f32)),
        in_specs=[VMEM] * 7, out_specs=[VMEM] * 2,
        compiler_params=PARAMS, cost_estimate=cost, name="back_keep",
    )(early, near, other, *shared)

    for r, pair in enumerate(rounds[::-1], 1):
        got = swap(send, *pair)
        if r < len(rounds):
            total = keep + got.astype(f32)
            part = total.shape[0] // 2
            keep, send = total[:part], total[part:].astype(bf16)
    sums, mass = pl.pallas_call(
        last_kernel,
        out_shape=(jax.ShapeDtypeStruct((owned, width), f32), jax.ShapeDtypeStruct((owned,), f32)),
        in_specs=[VMEM] * 2,
        out_specs=[VMEM, pl.BlockSpec(memory_space=pltpu.SMEM)],
        compiler_params=PARAMS, name="last",
    )(keep, got)
    return sums, mass, log_evidence[0]


def solution(mesh):
    placed = (
        P(("parts", "blk"), None),
        P(("parts", "blk"), None),
        P(("parts", "blk")),
        P(("parts", "blk"), None),
    )
    return jax.shard_map(
        local,
        mesh=mesh,
        in_specs=placed,
        out_specs=(P(("parts", "blk"), None), P(("parts", "blk")), P(("parts", "blk"))),
        check_vma=False,
    )
```
